256 devices in a mesh: row: 8 (over z), col: 32 (over y, x, core).
Axes of the slice: x: 4, y: 4, z: 8, core: 2. Of those that a mesh axis runs over, the one named last changes fastest.
Arguments:
- blocks: bfloat16 [8, 32, 256, 128, 128], P('row', 'col'), may hold values from 0 to 0.0625
- slot_rows: int32 [8, 32, 256], P('row', 'col'), may hold values from 0 to 255, as said below
- slot_cols: int32 [8, 32, 256], P('row', 'col'), may hold values from 0 to 63, as said below
- counts: int32 [8, 32], P('row', 'col'), may hold values from 0 to 256, as said below
- reward_table: bfloat16 [32, 262144], P('row', 'col'), may hold values from -6 to 6
- reward_cols: int32 [16], replicated, may hold values from 0 to 31, as said below
- cotangent: bfloat16 [16, 262144], P(None, ('row', 'col')), may hold values from -6 to 6
Outputs:
- value: float32 [16, 262144], P(None, ('row', 'col'))
- grad: float32 [16, 262144], P('row', 'col')
The draws below stay inside these ranges and needn't reach their ends.
Inputs may be any that keep to these rules, and one draw needn't show every extreme that they name: `counts`: stored blocks of each grid cell; along every grid row the cells of even index hold 2048 of them, and so do the cells of odd index, and some cell of every grid row holds exactly 256. Only the first counts[a, b] slots of a grid cell hold stored blocks; every block row has exactly 16 stored blocks; slot_rows[a, b, s] is even where b is even and odd where b is odd. `slot_cols`: two stored blocks at the same position add. `reward_cols`: distinct candidates.
All inputs are finite; a program needn't handle non-finite values.
Results may differ from the reference program's by a relative error of at most 0.0003.
Values may be sent and summed in bfloat16 or wider, within the bound.
A program may use at most 64 MiB of HBM per device.

```python
import jax
import jax.numpy as jnp
from jax import lax

BLK = 128
REWARDS = 16
CANDIDATES = 32
MEAN_DEV = 128
CAP = 256
SB_ROW = 256
SB_COL = 64
STATES = 262144
N_ROW = 8
N_COL = 32


def pattern(key):
    folded = jax.random.fold_in(key, 7001)
    subkeys = jax.random.split(folded, 4)
    half_cols = N_COL // 2
    quarter_cols = N_COL // 4
    half_rows = SB_ROW // 2
    swings = jax.random.randint(subkeys[0], (N_ROW, 2, quarter_cols), 0, MEAN_DEV + 1)
    swings = swings.at[:, :, 0].set(MEAN_DEV)
    paired = jnp.concatenate([MEAN_DEV + swings, MEAN_DEV - swings], axis=2)
    shuffle_keys = jax.random.split(subkeys[1], N_ROW * 2)
    shuffles = jax.vmap(lambda subkey: jax.random.permutation(subkey, half_cols))(shuffle_keys).reshape(N_ROW, 2, half_cols)
    grouped = jnp.take_along_axis(paired, shuffles, axis=2).astype(jnp.int32)
    starts = jnp.cumsum(grouped, axis=2) - grouped
    counts = jnp.transpose(grouped, (0, 2, 1)).reshape(N_ROW, N_COL)
    offsets = jnp.transpose(starts, (0, 2, 1)).reshape(N_ROW, N_COL)
    order_keys = jax.random.split(subkeys[2], N_ROW * 2)
    row_order = jax.vmap(lambda subkey: jax.random.permutation(subkey, half_rows))(order_keys).reshape(N_ROW, 2, half_rows)
    parity = jnp.arange(N_COL, dtype=jnp.int32) % 2
    cell_order = row_order[:, parity, :]
    serial = (offsets[:, :, None] + jnp.arange(CAP, dtype=jnp.int32)[None, None, :]) % half_rows
    pairs_index = jnp.take_along_axis(cell_order, serial, axis=2)
    slot_row_ids = 2 * pairs_index + parity[None, :, None]
    slot_col_ids = jax.random.randint(subkeys[3], (N_ROW, N_COL, CAP), 0, SB_COL)
    return (counts, slot_row_ids.astype(jnp.int32), slot_col_ids.astype(jnp.int32))


def draw_counts(key, part):
    return pattern(key)[0]


def draw_slot_rows(key, part):
    return pattern(key)[1]


def draw_slot_cols(key, part):
    return pattern(key)[2]


def draw_reward_cols(key, part):
    chosen = jax.random.permutation(jax.random.fold_in(key, 7003), CANDIDATES)
    return chosen[:REWARDS].astype(jnp.int32)


def block_scale(own_key, extent, shards, low, top_value):
    factor_of, own = 1.0, jax.random.fold_in(own_key, 6)
    for axis_at, parts in shards:
        heights = jnp.exp(jax.random.uniform(jax.random.fold_in(own, axis_at), (parts,), jnp.float32, low / len(shards), top_value / len(shards)))
        factor_of = factor_of * jnp.repeat(heights, extent[axis_at] // parts).reshape([-1 if axis == axis_at else 1 for axis in range(len(extent))])
    return factor_of


def noise(key, extent, width, most, cuts=(), kind=jnp.bfloat16):
    values = width * jax.random.normal(key, extent, jnp.float32)
    if cuts:
        values = values * block_scale(key, extent, cuts, -0.22, 0.18)
    return jnp.clip(values, -most, most).astype(kind)


def setup_inputs(seed: int = 0) -> dict:
    splits = jax.random.split(jax.random.key(seed), 8)
    blocks = jnp.clip(0.0625 * jax.random.uniform(splits[0], (N_ROW, N_COL, CAP, BLK, BLK), jnp.float32) ** block_scale(splits[0], (N_ROW, N_COL, CAP, BLK, BLK), ((0, 8), (1, 32)), -0.2, 0.2), 0.0, 0.0625).astype(jnp.bfloat16)
    slot_rows = draw_slot_rows(jax.random.fold_in(splits[7], 71), 0)
    slot_cols = draw_slot_cols(jax.random.fold_in(splits[7], 71), 0)
    counts = draw_counts(jax.random.fold_in(splits[7], 71), 0)
    reward_table = noise(splits[4], (CANDIDATES, STATES), 1.0, 6.0, ((0, 8), (1, 32)))
    reward_cols = draw_reward_cols(jax.random.fold_in(splits[7], 71), 0)
    cotangent = noise(splits[6], (REWARDS, STATES), 1.0, 6.0, ((1, 256),))
    return {"blocks": blocks, "slot_rows": slot_rows, "slot_cols": slot_cols, "counts": counts, "reward_table": reward_table, "reward_cols": reward_cols, "cotangent": cotangent}


def reference(blocks, slot_rows, slot_cols, counts, reward_table, reward_cols, cotangent):
    rewards = jnp.take(reward_table, reward_cols, axis=0)
    reward_cells = rewards.reshape(REWARDS, N_COL, SB_COL, BLK).astype(jnp.float32)
    weight_cells = cotangent.reshape(REWARDS, N_ROW, SB_ROW, BLK).astype(jnp.float32)
    slot_index = jnp.arange(CAP, dtype=jnp.int32)

    def visit(totals, cell_index):
        value_acc, grad_acc = totals
        grid_row = cell_index // N_COL
        grid_col = cell_index % N_COL
        stored = blocks[grid_row, grid_col].astype(jnp.float32)
        rows_here = slot_rows[grid_row, grid_col]
        cols_here = slot_cols[grid_row, grid_col]
        live_mask = (slot_index < counts[grid_row, grid_col]).astype(jnp.float32)[None, :, None]
        picked = jnp.take(reward_cells[:, grid_col], cols_here, axis=1)
        forward = jnp.einsum("kgc,grc->kgr", picked, stored) * live_mask
        value_acc = value_acc.at[:, grid_row, rows_here].add(forward)
        weights = jnp.take(weight_cells[:, grid_row], rows_here, axis=1)
        backward = jnp.einsum("kgr,grc->kgc", weights, stored) * live_mask
        grad_acc = grad_acc.at[:, grid_col, cols_here].add(backward)
        return (value_acc, grad_acc), None

    start_values = jnp.zeros((REWARDS, N_ROW, SB_ROW, BLK), jnp.float32)
    start_grads = jnp.zeros((REWARDS, N_COL, SB_COL, BLK), jnp.float32)
    cells = jnp.arange(N_ROW * N_COL, dtype=jnp.int32)
    (value_acc, grad_acc), _ = lax.scan(visit, (start_values, start_grads), cells)
    return value_acc.reshape(REWARDS, STATES), grad_acc.reshape(REWARDS, STATES)
```

```python
import functools

import jax
import jax.numpy as jnp
from jax import lax
from jax.experimental import pallas as pl
from jax.experimental.pallas import tpu as pltpu
from jax.sharding import PartitionSpec as P

F32 = jnp.float32
BF16 = jnp.bfloat16
MESH = pl.DeviceIdType.MESH
NT = (((1,), (1,)), ((), ()))
NZ = 8
NX = 4
NY = 4
VMEM_BYTES = 48 << 20
UNROLL = 32
CHUNKS = 8


def position():
    z = lax.axis_index("row")
    col = lax.axis_index("col")
    return z, lax.rem(lax.div(col, 2), NX), lax.div(col, 2 * NX), lax.rem(col, 2)


def device(z, x, y, core):
    return (z, (y * NX + x) * 2 + core)


def plane_peers(z, x, y, core):
    peers = [device(z, x, y, 1 - core)]
    for i in range(1, NX):
        for c in range(2):
            peers.append(device(z, lax.rem(x + i, NX), y, c))
            peers.append(device(z, x, lax.rem(y + i, NY), c))
    return peers


def barrier(peers):
    semaphore = pltpu.get_barrier_semaphore()
    for peer in peers:
        pl.semaphore_signal(semaphore, inc=1, device_id=peer, device_id_type=MESH)
    pl.semaphore_wait(semaphore, len(peers))


def remote(src, dst, send, recv, peer):
    return pltpu.make_async_remote_copy(
        src_ref=src, dst_ref=dst, send_sem=send, recv_sem=recv, device_id=peer, device_id_type=MESH
    )


def gather_kernel(
    table, cols, cot, rew_out, w_out,
    tab, tabf, own_cot, full, sel, w, cols_s,
    load_sem, zsend, zrecv, psend, precv, qsend, qrecv,
):
    z, x, y, core = position()
    chip = y * NX + x
    loads = [
        pltpu.make_async_copy(table, tab, load_sem.at[0]),
        pltpu.make_async_copy(cols, cols_s, load_sem.at[1]),
    ]
    for t in range(8):
        loads.append(
            pltpu.make_async_copy(
                cot.at[:, pl.ds(t * 128, 128)], own_cot.at[t % 2, t // 2], load_sem.at[2 + t]
            )
        )
    for load in loads:
        load.start()
    up = device(lax.rem(z + 1, NZ), x, y, core)
    down = device(lax.rem(z + NZ - 1, NZ), x, y, core)
    semaphore = pltpu.get_barrier_semaphore()
    peers = [up, down] + plane_peers(z, x, y, core)
    for peer in peers:
        pl.semaphore_signal(semaphore, inc=1, device_id=peer, device_id_type=MESH)
    loads[0].wait()
    for j in range(64):
        tabf[pl.ds(j, 4, stride=64), :] = tab[:, j * 128 : (j + 1) * 128].astype(F32)
    for r in range(4):
        full[z * 4 + r] = tabf[r * 64 : (r + 1) * 64].astype(BF16)
    pl.semaphore_wait(semaphore, len(peers))

    def hop(d, r, way):
        back = lax.rem(z + NZ - (d - 1), NZ) if way == 0 else lax.rem(z + d - 1, NZ)
        piece = full.at[back * 4 + r]
        at = (way, d - 1, r)
        return remote(piece, piece, zsend.at[at], zrecv.at[at], up if way == 0 else down)

    def arrived(d, r, way):
        origin = lax.rem(z + NZ - d, NZ) if way == 0 else lax.rem(z + d, NZ)
        piece = full.at[origin * 4 + r]
        at = (way, d - 1, r)
        return remote(piece, piece, zsend.at[at], zrecv.at[at], up if way == 0 else down)

    def ways(d, r):
        return (0, 1) if d < 4 else ((0,) if r < 2 else (1,))

    for r in range(4):
        for way in ways(1, r):
            hop(1, r, way).start()
    for load in loads[2:]:
        load.wait()

    first = []
    for i in range(NX):
        tx = lax.rem(x + i * (1 - core), NX)
        ty = lax.rem(y + i * core, NY)
        for c in range(2):
            if i == 0:
                if c == 0:
                    first.append(
                        remote(
                            own_cot.at[1 - core], w.at[y, x, core],
                            psend.at[0, 0], precv.at[core, 0], device(z, x, y, 1 - core),
                        )
                    )
                continue
            first.append(
                remote(
                    own_cot.at[c], w.at[y, x, core],
                    psend.at[i, c], precv.at[core, i], device(z, tx, ty, c),
                )
            )
    for copy in first:
        copy.start()
    mine = pltpu.make_async_copy(own_cot.at[core], w.at[y, x, core], load_sem.at[1])
    loads[1].wait()
    mine.start()

    for r in range(4):
        for way in ways(1, r):
            arrived(1, r, way).wait_recv()
            if way in ways(2, r):
                hop(2, r, way).start()

    def first_arrived(i, half):
        piece = w.at[lax.rem(y + NY - i * half, NY), lax.rem(x + NX - i * (1 - half), NX), half]
        return remote(own_cot.at[0], piece, psend.at[0, 0], precv.at[half, i], device(z, x, y, 1 - core))

    mine.wait()
    remote(
        own_cot.at[0], w.at[y, x, 1 - core], psend.at[0, 0], precv.at[1 - core, 0], device(z, x, y, 1 - core)
    ).wait_recv()
    for i in range(1, NX):
        for half in range(2):
            first_arrived(i, half).wait_recv()

    second = []
    for i in range(1, NX):
        second.append(
            remote(
                w.at[y, :, 0], w.at[y, :, 0], qsend.at[0, i], qrecv.at[0, i],
                device(z, x, lax.rem(y + i, NY), core),
            )
        )
        second.append(
            remote(
                w.at[:, x, 1], w.at[:, x, 1], qsend.at[1, i], qrecv.at[1, i],
                device(z, lax.rem(x + i, NX), y, core),
            )
        )
    for copy in second:
        copy.start()

    for d in (2, 3):
        for r in range(4):
            for way in ways(d, r):
                arrived(d, r, way).wait_recv()
                if way in ways(d + 1, r):
                    hop(d + 1, r, way).start()
    for i in range(1, NX):
        sy = lax.rem(y + NY - i, NY)
        sx = lax.rem(x + NX - i, NX)
        remote(w.at[sy, :, 0], w.at[sy, :, 0], qsend.at[0, i], qrecv.at[0, i], up).wait_recv()
        remote(w.at[:, sx, 1], w.at[:, sx, 1], qsend.at[1, i], qrecv.at[1, i], up).wait_recv()
    w_out[...] = w[...].reshape(w_out.shape)
    for r in range(4):
        for way in ways(4, r):
            arrived(4, r, way).wait_recv()
    for k in range(16):
        sel[k * 64 : (k + 1) * 64] = full[cols_s[k]].astype(F32)
    for j in range(64):
        rew_out[j] = sel[pl.ds(j, 16, stride=64), :].astype(BF16)
    for d in (1, 2, 3, 4):
        for r in range(4):
            for way in ways(d, r):
                hop(d, r, way).wait_send()
    for copy in first + second:
        copy.wait_send()


def gather(table, cols, cot):
    anywhere = pl.BlockSpec(memory_space=pl.ANY)
    vmem = pl.BlockSpec(memory_space=pltpu.VMEM)
    dma = pltpu.SemaphoreType.DMA
    return pl.pallas_call(
        gather_kernel,
        out_shape=(
            jax.ShapeDtypeStruct((64, 16, 128), BF16),
            jax.ShapeDtypeStruct((128, 16, 128), BF16),
        ),
        in_specs=[anywhere] * 3,
        out_specs=(vmem, vmem),
        scratch_shapes=[
            pltpu.VMEM((4, 8192), BF16),
            pltpu.VMEM((256, 128), F32),
            pltpu.VMEM((2, 4, 16, 128), BF16),
            pltpu.VMEM((32, 64, 128), BF16),
            pltpu.VMEM((1024, 128), F32),
            pltpu.VMEM((NY, NX, 2, 4, 16, 128), BF16),
            pltpu.SMEM((16,), jnp.int32),
            dma((10,)),
            dma((2, 4, 4)),
            dma((2, 4, 4)),
            dma((4, 2)),
            dma((2, 4)),
            dma((2, 4)),
            dma((2, 4)),
        ],
        compiler_params=pltpu.CompilerParams(
            collective_id=0, has_side_effects=True, vmem_limit_bytes=VMEM_BYTES
        ),
    )(table, cols, cot)


def product_kernel(
    slot_rows, slot_cols, counts, blocks, rew, w, val, grad_rows,
    rows_s, cols_s, count_s, stored, grad, sem,
):
    each = 256 // CHUNKS
    small = [
        pltpu.make_async_copy(slot_rows, rows_s, sem.at[CHUNKS]),
        pltpu.make_async_copy(slot_cols, cols_s, sem.at[CHUNKS + 1]),
        pltpu.make_async_copy(counts, count_s, sem.at[CHUNKS + 2]),
    ]
    large = [
        pltpu.make_async_copy(
            blocks.at[0, 0, pl.ds(i * each, each)], stored.at[pl.ds(i * each, each)], sem.at[i]
        )
        for i in range(CHUNKS)
    ]
    for copy in small + large:
        copy.start()
    val[...] = jnp.zeros_like(val)
    grad[...] = jnp.zeros_like(grad)
    for copy in small:
        copy.wait()
    live = count_s[0, 0]
    zero = jnp.zeros((16, 128), BF16)
    for i in range(CHUNKS):
        large[i].wait()

        @pl.loop(i * each, (i + 1) * each, step=UNROLL)
        def _(start):
            places, forward, adjoint = [], [], []
            for u in range(0, UNROLL, 2):
                s = start + u
                pair = stored[pl.ds(s, 2)].reshape(256, 128)
                r0, r1 = lax.div(rows_s[0, 0, s], 2), lax.div(rows_s[0, 0, s + 1], 2)
                c0, c1 = cols_s[0, 0, s], cols_s[0, 0, s + 1]
                m0, m1 = (s < live).astype(F32), (s + 1 < live).astype(F32)
                left = jnp.concatenate([rew[c0], rew[c1]], axis=0)
                out = lax.dot_general(left, pair, NT, preferred_element_type=F32)
                forward += [out[:16, :128] * m0, out[16:, 128:] * m1]
                left = jnp.concatenate(
                    [
                        jnp.concatenate([w[r0], zero], axis=1),
                        jnp.concatenate([zero, w[r1]], axis=1),
                    ],
                    axis=0,
                )
                out = jnp.dot(left, pair, preferred_element_type=F32)
                adjoint += [out[:16] * m0, out[16:] * m1]
                places += [(r0, c0), (r1, c1)]
            for u, (r, c) in enumerate(places):
                val[r] += forward[u]
                grad[pl.ds(c * 16, 16)] += adjoint[u]

    for k in range(16):
        grad_rows[k] = grad[pl.ds(k, 64, stride=16), :]


def products(slot_rows, slot_cols, counts, blocks, rew, w):
    anywhere = pl.BlockSpec(memory_space=pl.ANY)
    vmem = pl.BlockSpec(memory_space=pltpu.VMEM)
    return pl.pallas_call(
        product_kernel,
        out_shape=(
            jax.ShapeDtypeStruct((128, 16, 128), F32),
            jax.ShapeDtypeStruct((16, 64, 128), F32),
        ),
        in_specs=[anywhere] * 4 + [vmem] * 2,
        out_specs=(vmem, vmem),
        scratch_shapes=[
            pltpu.SMEM((1, 1, 256), jnp.int32),
            pltpu.SMEM((1, 1, 256), jnp.int32),
            pltpu.SMEM((1, 1), jnp.int32),
            pltpu.VMEM((256, 128, 128), BF16),
            pltpu.VMEM((1024, 128), F32),
            pltpu.SemaphoreType.DMA((CHUNKS + 3,)),
        ],
        compiler_params=pltpu.CompilerParams(vmem_limit_bytes=VMEM_BYTES),
    )(slot_rows, slot_cols, counts, blocks, rew, w)


def scatter_kernel(
    val, grad_rows, value_out, grad_out,
    zbuf, zin, abuf, bbuf, asum, bsum, fin, gsum,
    zsend, zrecv, psend, precv, qsend, qrecv,
):
    z, x, y, core = position()
    up = device(lax.rem(z + 1, NZ), x, y, core)
    down = device(lax.rem(z + NZ - 1, NZ), x, y, core)
    barrier([up, down] + plane_peers(z, x, y, core))

    def owner(way, d):
        return lax.rem(z + d, NZ) if way == 0 else lax.rem(z + NZ - d, NZ)

    def send(way, d, r, first):
        at = (way, d - 1, r)
        src = grad_rows.at[owner(way, d) * 2 + r] if first else zbuf.at[at]
        return remote(src, zin.at[at], zsend.at[at], zrecv.at[at], up if way == 0 else down)

    far = {(0, 0): 4, (0, 1): 3, (1, 0): 3, (1, 1): 4}
    for r in (0, 1):
        for way in (0, 1):
            send(way, far[way, r], r, True).start()

    first = []
    for i in range(1, NX):
        tx = lax.rem(x + i, NX)
        ty = lax.rem(y + i, NY)
        first.append(
            remote(val.at[:, tx, 0], abuf.at[i - 1], psend.at[0, i - 1], precv.at[0, i - 1], device(z, tx, y, core))
        )
        first.append(
            remote(val.at[ty, :, 1], bbuf.at[i - 1], psend.at[1, i - 1], precv.at[1, i - 1], device(z, x, ty, core))
        )
    for copy in first:
        copy.start()

    def relay(d):
        for way in (0, 1):
            for r in (0, 1):
                if d + 1 > far[way, r]:
                    continue
                send(way, d + 1, r, False).wait_recv()
                at = (way, d - 1, r)
                zbuf[at] = zin[way, d, r] + grad_rows[owner(way, d) * 2 + r]
                send(way, d, r, False).start()

    relay(3)
    relay(2)
    for copy in first:
        copy.wait_recv()
    asum[...] = val[:, x, 0] + abuf[0] + abuf[1] + abuf[2]
    bsum[...] = val[y, :, 1] + bbuf[0] + bbuf[1] + bbuf[2]

    second = []
    for i in range(1, NX):
        ty = lax.rem(y + i, NY)
        tx = lax.rem(x + i, NX)
        second.append(
            remote(asum.at[ty], fin.at[core, i], qsend.at[0, i], qrecv.at[core, i], device(z, x, ty, 0))
        )
        second.append(
            remote(bsum.at[tx], fin.at[core, i], qsend.at[1, i], qrecv.at[core, i], device(z, tx, y, 1))
        )
    for copy in second:
        copy.start()
    partner = device(z, x, y, 1 - core)

    @pl.when(core == 0)
    def _():
        remote(bsum.at[x], fin.at[core, 0], qsend.at[0, 0], qrecv.at[core, 0], partner).start()
        fin[core, 0] = asum[y]

    @pl.when(core == 1)
    def _():
        remote(asum.at[y], fin.at[core, 0], qsend.at[0, 0], qrecv.at[core, 0], partner).start()
        fin[core, 0] = bsum[x]

    relay(1)
    last = remote(asum.at[0], fin.at[1 - core, 0], qsend.at[0, 0], qrecv.at[1 - core, 0], partner)
    last.wait_recv()
    for c in range(2):
        for i in range(1, NX):
            remote(asum.at[0], fin.at[c, i], qsend.at[0, i], qrecv.at[c, i], partner).wait_recv()
    for t in range(8):
        p, h = t % 2, t // 2
        value_out[:, t * 128 : (t + 1) * 128] = fin[p, 0, h] + fin[p, 1, h] + fin[p, 2, h] + fin[p, 3, h]
    for way in (0, 1):
        for r in (0, 1):
            send(way, 1, r, False).wait_recv()
    for r in (0, 1):
        gsum[r * 64 : (r + 1) * 64] = grad_rows[z * 2 + r] + zin[0, 0, r] + zin[1, 0, r]
    for j in range(64):
        grad_out[:, j * 128 : (j + 1) * 128] = gsum[pl.ds(j, 2, stride=64), :]
    for way in (0, 1):
        for r in (0, 1):
            for d in range(1, far[way, r] + 1):
                send(way, d, r, d == far[way, r]).wait_send()
    for copy in first + second:
        copy.wait_send()
    last.wait_send()


def scatter(val, grad_rows):
    vmem = pl.BlockSpec(memory_space=pltpu.VMEM)
    dma = pltpu.SemaphoreType.DMA
    return pl.pallas_call(
        scatter_kernel,
        out_shape=(jax.ShapeDtypeStruct((16, 1024), F32), jax.ShapeDtypeStruct((2, 8192), F32)),
        in_specs=[vmem, vmem],
        out_specs=(vmem, vmem),
        scratch_shapes=[
            pltpu.VMEM((2, 4, 2, 64, 128), F32),
            pltpu.VMEM((2, 4, 2, 64, 128), F32),
            pltpu.VMEM((3, 4, 4, 16, 128), F32),
            pltpu.VMEM((3, 4, 4, 16, 128), F32),
            pltpu.VMEM((4, 4, 16, 128), F32),
            pltpu.VMEM((4, 4, 16, 128), F32),
            pltpu.VMEM((2, 4, 4, 16, 128), F32),
            pltpu.VMEM((128, 128), F32),
            dma((2, 4, 2)),
            dma((2, 4, 2)),
            dma((2, 3)),
            dma((2, 3)),
            dma((2, 4)),
            dma((2, 4)),
        ],
        compiler_params=pltpu.CompilerParams(
            collective_id=1, has_side_effects=True, vmem_limit_bytes=VMEM_BYTES
        ),
    )(val, grad_rows)


def on_device(blocks, slot_rows, slot_cols, counts, reward_table, reward_cols, cotangent):
    rew, w = gather(reward_table, reward_cols, cotangent)
    val, grad_rows = products(slot_rows, slot_cols, counts, blocks, rew, w)
    return scatter(val.reshape(NY, NX, 2, 4, 16, 128), grad_rows)


def solution(mesh):
    placed = (
        P("row", "col", None, None, None),
        P("row", "col", None),
        P("row", "col", None),
        P("row", "col"),
        P("row", "col"),
        P(),
        P(None, ("row", "col")),
    )
    return jax.shard_map(
        on_device,
        mesh=mesh,
        in_specs=placed,
        out_specs=(P(None, ("row", "col")), P("row", "col")),
        check_vma=False,
    )
```

```python
import functools

import jax
import jax.numpy as jnp
from jax import lax
from jax.experimental import pallas as pl
from jax.experimental.pallas import tpu as pltpu
from jax.sharding import PartitionSpec as P

F32 = jnp.float32
BF16 = jnp.bfloat16
MESH = pl.DeviceIdType.MESH
NT = (((1,), (1,)), ((), ()))
NZ = 8
NX = 4
NY = 4
VMEM_BYTES = 62 << 20
UNROLL = 64
CHUNKS = 8


def position():
    z = lax.axis_index("row")
    col = lax.axis_index("col")
    return z, lax.rem(lax.div(col, 2), NX), lax.div(col, 2 * NX), lax.rem(col, 2)


def device(z, x, y, core):
    return (z, (y * NX + x) * 2 + core)


def plane_peers(z, x, y, core):
    peers = [device(z, x, y, 1 - core)]
    for i in range(1, NX):
        for c in range(2):
            peers.append(device(z, lax.rem(x + i, NX), y, c))
            peers.append(device(z, x, lax.rem(y + i, NY), c))
    return peers


def remote(src, dst, send, recv, peer):
    return pltpu.make_async_remote_copy(
        src_ref=src, dst_ref=dst, send_sem=send, recv_sem=recv, device_id=peer, device_id_type=MESH
    )


def one_hot(index, height, live, target):
    rows = lax.broadcasted_iota(jnp.int32, (height, 256), 0)
    slots = lax.broadcasted_iota(jnp.int32, (height, 256), 1)
    hit = (target(rows) == index) & (slots < live)
    return jnp.where(hit, 1.0, 0.0).astype(BF16)


def slot_sums(hot, products, k):
    part = products[pl.ds(k, 256, stride=16), :]
    high = part.astype(BF16)
    low = (part - high.astype(F32)).astype(BF16)
    out = jnp.dot(hot, jnp.concatenate([high, low], axis=1), preferred_element_type=F32)
    return out[:, :128] + out[:, 128:]


def kernel(
    blocks, slot_rows, slot_cols, counts, table, reward_cols, cot, value_out, grad_out,
    stored, rows_s, cols_s, count_s, picks_s, rows_v, cols_v,
    tab, tabf, own_cot, full, sel, rew, w, wf, hot_rows, hot_cols,
    adjoint, forward, vsum, vtile, grads, gsum,
    abuf, bbuf, asum, bsum, fin, near, mid, far, relay,
    load_sem, block_sem, gsend, grecv, psend, precv, qsend, qrecv,
    zsend, zrecv, vsend, vrecv, fsend, frecv,
):
    z, x, y, core = position()
    partner = device(z, x, y, 1 - core)

    def along_z(step):
        return device(lax.rem(z + NZ + step, NZ), x, y, core)

    def at_z(step):
        return lax.rem(z + NZ + step, NZ)

    loads = [
        pltpu.make_async_copy(table, tab, load_sem.at[0]),
        pltpu.make_async_copy(reward_cols, picks_s, load_sem.at[1]),
        pltpu.make_async_copy(slot_rows, rows_s, load_sem.at[2]),
        pltpu.make_async_copy(slot_cols, cols_s, load_sem.at[3]),
        pltpu.make_async_copy(counts, count_s, load_sem.at[4]),
        pltpu.make_async_copy(slot_rows, rows_v, load_sem.at[5]),
        pltpu.make_async_copy(slot_cols, cols_v, load_sem.at[6]),
    ]
    cot_loads = [
        pltpu.make_async_copy(cot.at[:, pl.ds(t * 128, 128)], own_cot.at[t % 2, t // 2], load_sem.at[7 + t])
        for t in range(8)
    ]
    each = 256 // CHUNKS
    block_loads = [
        pltpu.make_async_copy(
            blocks.at[0, 0, pl.ds(i * each, each)], stored.at[pl.ds(i * each, each)], block_sem.at[i]
        )
        for i in range(CHUNKS)
    ]
    for load in loads[:1] + cot_loads + loads[1:] + block_loads:
        load.start()
    semaphore = pltpu.get_barrier_semaphore()
    peers = [along_z(2), along_z(-2), along_z(1), along_z(-1)] + plane_peers(z, x, y, core)
    for peer in peers:
        pl.semaphore_signal(semaphore, inc=1, device_id=peer, device_id_type=MESH)
    loads[0].wait()
    for j in range(64):
        tabf[pl.ds(j, 4, stride=64), :] = tab[:, j * 128 : (j + 1) * 128].astype(F32)
    for r in range(4):
        full[z * 4 + r] = tabf[r * 64 : (r + 1) * 64].astype(BF16)
    for load in cot_loads:
        load.wait()
    pl.semaphore_wait(semaphore, len(peers))

    def reward_copy(way, kind, half, receiving):
        sign = 1 if way == 0 else -1
        reach = (1, 2, 1, 2)[kind]
        origin = -sign * ((1, 2, 3, 4)[kind] if receiving else (0, 0, 2, 2)[kind])
        piece = full.at[pl.ds(at_z(origin) * 4 + half * 2, 2)]
        at = (way, kind, half)
        return remote(piece, piece, gsend.at[at], grecv.at[at], along_z(sign * reach))

    for kind in (1, 0):
        for half in (0, 1):
            for way in (0, 1):
                reward_copy(way, kind, half, False).start()

    first = [remote(own_cot.at[1 - core], w.at[y, x, core], psend.at[0, 0], precv.at[core, 0], partner)]
    for i in range(1, NX):
        tx = lax.rem(x + i * (1 - core), NX)
        ty = lax.rem(y + i * core, NY)
        for c in range(2):
            first.append(
                remote(own_cot.at[c], w.at[y, x, core], psend.at[i, c], precv.at[core, i], device(z, tx, ty, c))
            )
    for copy in first:
        copy.start()
    w[y, x, core] = own_cot[core]

    for load in loads[1:]:
        load.wait()
    live = count_s[0, 0]

    def block_row(at):
        half, a, b, t = at >> 6, (at >> 4) & 3, (at >> 2) & 3, at & 3
        tx, ty = jnp.where(half == 0, a, b), jnp.where(half == 0, b, a)
        return ((ty * NX + tx) * 2 + half) * 8 + t * 2 + core

    hot_rows[...] = one_hot(rows_v[0], 128, live, block_row)
    hot_cols[...] = one_hot(cols_v[0], 64, live, lambda at: at)

    remote(own_cot.at[0], w.at[y, x, 1 - core], psend.at[0, 0], precv.at[1 - core, 0], partner).wait_recv()
    for i in range(1, NX):
        for half in range(2):
            piece = w.at[lax.rem(y + NY - i * half, NY), lax.rem(x + NX - i * (1 - half), NX), half]
            remote(own_cot.at[0], piece, psend.at[0, 0], precv.at[half, i], partner).wait_recv()

    second = []
    for i in range(1, NX):
        row, column = w.at[y, :, 0], w.at[:, x, 1]
        second.append(
            remote(row, row, qsend.at[0, i], qrecv.at[0, i], device(z, x, lax.rem(y + i, NY), core))
        )
        second.append(
            remote(column, column, qsend.at[1, i], qrecv.at[1, i], device(z, lax.rem(x + i, NX), y, core))
        )
    for copy in second:
        copy.start()

    for half in (0, 1):
        for way in (0, 1):
            reward_copy(way, 1, half, True).wait_recv()
            reward_copy(way, 2, half, False).start()
            if half == way:
                reward_copy(way, 3, half, False).start()

    for i in range(1, NX):
        row, column = w.at[lax.rem(y + NY - i, NY), :, 0], w.at[:, lax.rem(x + NX - i, NX), 1]
        remote(row, row, qsend.at[0, i], qrecv.at[0, i], partner).wait_recv()
        remote(column, column, qsend.at[1, i], qrecv.at[1, i], partner).wait_recv()
    wf[...] = w[...].reshape(wf.shape)
    for load in block_loads:
        load.wait()

    zero = jnp.zeros((16, 128), BF16)

    @pl.loop(0, 256, step=UNROLL)
    def _(start):
        for u in range(0, UNROLL, 2):
            s = start + u
            pair = stored[pl.ds(s, 2)].reshape(256, 128)
            w0 = wf[lax.div(rows_s[0, 0, s], 2)]
            w1 = wf[lax.div(rows_s[0, 0, s + 1], 2)]
            left = jnp.concatenate(
                [jnp.concatenate([w0, zero], axis=1), jnp.concatenate([zero, w1], axis=1)], axis=0
            )
            adjoint[pl.ds(pl.multiple_of(s * 16, 32), 32), :] = jnp.dot(left, pair, preferred_element_type=F32)

    for k in range(16):
        grads[k] = slot_sums(hot_cols[...], adjoint, k)

    def sign_of(way):
        return 1 if way == 0 else -1

    def far_copy(way):
        s = sign_of(way)
        return remote(
            grads.at[at_z(4) * 2 + way], far.at[way], zsend.at[way, 0], zrecv.at[way, 0], along_z(2 * s)
        )

    def mid_copy(way):
        s = sign_of(way)
        return remote(
            grads.at[pl.ds(at_z(3 * s) * 2, 2)], mid.at[way], zsend.at[way, 1], zrecv.at[way, 1], along_z(s)
        )

    def near_copy(way):
        s = sign_of(way)
        return remote(
            grads.at[pl.ds(at_z(s) * 2, 2)], near.at[0, way], zsend.at[way, 2], zrecv.at[way, 2], along_z(s)
        )

    def relay_copy(way):
        s = sign_of(way)
        return remote(relay.at[way], near.at[1, way], zsend.at[way, 3], zrecv.at[way, 3], along_z(2 * s))

    for copy in (far_copy, mid_copy, near_copy):
        for way in (0, 1):
            copy(way).start()

    for way in (0, 1):
        for half in (0, 1):
            reward_copy(way, 0, half, True).wait_recv()
            reward_copy(way, 2, half, True).wait_recv()
        reward_copy(way, 3, way, True).wait_recv()
    for k in range(16):
        sel[k * 64 : (k + 1) * 64] = full[picks_s[k]].astype(F32)
    for j in range(64):
        rew[j] = sel[pl.ds(j, 16, stride=64), :].astype(BF16)

    @pl.loop(0, 256, step=UNROLL)
    def _(start):
        for u in range(0, UNROLL, 2):
            s = start + u
            pair = stored[pl.ds(s, 2)].reshape(256, 128)
            left = jnp.concatenate([rew[cols_s[0, 0, s]], rew[cols_s[0, 0, s + 1]]], axis=0)
            out = lax.dot_general(left, pair, NT, preferred_element_type=F32)
            at = pl.multiple_of(s * 16, 32)
            forward[pl.ds(at, 16), :] = out[:16, :128]
            forward[pl.ds(at + 16, 16), :] = out[16:, 128:]

    for k in range(16):
        vsum[k * 128 : (k + 1) * 128] = slot_sums(hot_rows[...], forward, k)
    for i in range(128):
        vtile[i >> 6, (i >> 4) & 3, (i >> 2) & 3, i & 3] = vsum[pl.ds(i, 16, stride=128), :]

    value_first = []
    for i in range(1, NX):
        tx = lax.rem(x + i, NX)
        ty = lax.rem(y + i, NY)
        value_first.append(
            remote(vtile.at[0, tx], abuf.at[i - 1], vsend.at[0, i - 1], vrecv.at[0, i - 1], device(z, tx, y, core))
        )
        value_first.append(
            remote(vtile.at[1, ty], bbuf.at[i - 1], vsend.at[1, i - 1], vrecv.at[1, i - 1], device(z, x, ty, core))
        )
    for copy in value_first:
        copy.start()

    for way in (0, 1):
        mid_copy(way).wait_recv()
        far_copy(way).wait_recv()
        s = sign_of(way)
        relay[way] = grads[pl.ds(at_z(2 * s) * 2, 2)] + mid[way]
        relay[way, way] = relay[way, way] + far[way]
        relay_copy(way).start()

    for copy in value_first:
        copy.wait_recv()
    asum[...] = vtile[0, x] + abuf[0] + abuf[1] + abuf[2]
    bsum[...] = vtile[1, y] + bbuf[0] + bbuf[1] + bbuf[2]

    value_second = []
    for i in range(1, NX):
        ty = lax.rem(y + i, NY)
        tx = lax.rem(x + i, NX)
        value_second.append(
            remote(asum.at[ty], fin.at[core, i], fsend.at[0, i], frecv.at[core, i], device(z, x, ty, 0))
        )
        value_second.append(
            remote(bsum.at[tx], fin.at[core, i], fsend.at[1, i], frecv.at[core, i], device(z, tx, y, 1))
        )
    for copy in value_second:
        copy.start()

    @pl.when(core == 0)
    def _():
        remote(bsum.at[x], fin.at[core, 0], fsend.at[0, 0], frecv.at[core, 0], partner).start()
        fin[core, 0] = asum[y]

    @pl.when(core == 1)
    def _():
        remote(asum.at[y], fin.at[core, 0], fsend.at[0, 0], frecv.at[core, 0], partner).start()
        fin[core, 0] = bsum[x]

    for way in (0, 1):
        near_copy(way).wait_recv()
        relay_copy(way).wait_recv()
    for r in (0, 1):
        gsum[r * 64 : (r + 1) * 64] = (
            grads[z * 2 + r] + near[0, 0, r] + near[0, 1, r] + near[1, 0, r] + near[1, 1, r]
        )
    for j in range(64):
        grad_out[:, j * 128 : (j + 1) * 128] = gsum[pl.ds(j, 2, stride=64), :]

    last = remote(asum.at[0], fin.at[1 - core, 0], fsend.at[0, 0], frecv.at[1 - core, 0], partner)
    last.wait_recv()
    for c in range(2):
        for i in range(1, NX):
            remote(asum.at[0], fin.at[c, i], fsend.at[0, i], frecv.at[c, i], partner).wait_recv()
    for t in range(8):
        p, h = t % 2, t // 2
        value_out[:, t * 128 : (t + 1) * 128] = fin[p, 0, h] + fin[p, 1, h] + fin[p, 2, h] + fin[p, 3, h]

    for way in (0, 1):
        for half in (0, 1):
            for kind in (0, 1, 2):
                reward_copy(way, kind, half, False).wait_send()
        reward_copy(way, 3, way, False).wait_send()
        for copy in (far_copy, mid_copy, near_copy, relay_copy):
            copy(way).wait_send()
    for copy in first + second + value_first + value_second + [last]:
        copy.wait_send()


def on_device(*operands):
    vmem = pl.BlockSpec(memory_space=pltpu.VMEM)
    dma = pltpu.SemaphoreType.DMA
    return pl.pallas_call(
        kernel,
        out_shape=(jax.ShapeDtypeStruct((16, 1024), F32), jax.ShapeDtypeStruct((2, 8192), F32)),
        in_specs=[pl.BlockSpec(memory_space=pltpu.HBM)] * 7,
        out_specs=(vmem, vmem),
        scratch_shapes=[
            pltpu.VMEM((256, 128, 128), BF16),
            pltpu.SMEM((1, 1, 256), jnp.int32),
            pltpu.SMEM((1, 1, 256), jnp.int32),
            pltpu.SMEM((1, 1), jnp.int32),
            pltpu.SMEM((16,), jnp.int32),
            pltpu.VMEM((1, 1, 256), jnp.int32),
            pltpu.VMEM((1, 1, 256), jnp.int32),
            pltpu.VMEM((4, 8192), BF16),
            pltpu.VMEM((256, 128), F32),
            pltpu.VMEM((2, 4, 16, 128), BF16),
            pltpu.VMEM((32, 64, 128), BF16),
            pltpu.VMEM((1024, 128), F32),
            pltpu.VMEM((64, 16, 128), BF16),
            pltpu.VMEM((NY, NX, 2, 4, 16, 128), BF16),
            pltpu.VMEM((128, 16, 128), BF16),
            pltpu.VMEM((128, 256), BF16),
            pltpu.VMEM((64, 256), BF16),
            pltpu.VMEM((4096, 128), F32),
            pltpu.VMEM((4096, 128), F32),
            pltpu.VMEM((2048, 128), F32),
            pltpu.VMEM((2, 4, 4, 4, 16, 128), F32),
            pltpu.VMEM((16, 64, 128), F32),
            pltpu.VMEM((128, 128), F32),
            pltpu.VMEM((3, 4, 4, 16, 128), F32),
            pltpu.VMEM((3, 4, 4, 16, 128), F32),
            pltpu.VMEM((4, 4, 16, 128), F32),
            pltpu.VMEM((4, 4, 16, 128), F32),
            pltpu.VMEM((2, 4, 4, 16, 128), F32),
            pltpu.VMEM((2, 2, 2, 64, 128), F32),
            pltpu.VMEM((2, 2, 64, 128), F32),
            pltpu.VMEM((2, 64, 128), F32),
            pltpu.VMEM((2, 2, 64, 128), F32),
            dma((15,)),
            dma((CHUNKS,)),
            dma((2, 4, 2)),
            dma((2, 4, 2)),
            dma((4, 2)),
            dma((2, 4)),
            dma((2, 4)),
            dma((2, 4)),
            dma((2, 4)),
            dma((2, 4)),
            dma((2, 3)),
            dma((2, 3)),
            dma((2, 4)),
            dma((2, 4)),
        ],
        compiler_params=pltpu.CompilerParams(
            collective_id=0, has_side_effects=True, vmem_limit_bytes=VMEM_BYTES
        ),
    )(*operands)


def solution(mesh):
    placed = (
        P("row", "col", None, None, None),
        P("row", "col", None),
        P("row", "col", None),
        P("row", "col"),
        P("row", "col"),
        P(),
        P(None, ("row", "col")),
    )
    return jax.shard_map(
        on_device,
        mesh=mesh,
        in_specs=placed,
        out_specs=(P(None, ("row", "col")), P("row", "col")),
        check_vma=False,
    )
```

```python
import functools

import jax
import jax.numpy as jnp
from jax import lax
from jax.experimental import pallas as pl
from jax.experimental.pallas import tpu as pltpu
from jax.sharding import PartitionSpec as P

F32 = jnp.float32
BF16 = jnp.bfloat16
MESH = pl.DeviceIdType.MESH
NT = (((1,), (1,)), ((), ()))
NZ = 8
NX = 4
NY = 4
VMEM_BYTES = 48 << 20
UNROLL = 64
CHUNKS = 8


def position():
    z = lax.axis_index("row")
    col = lax.axis_index("col")
    return z, lax.rem(lax.div(col, 2), NX), lax.div(col, 2 * NX), lax.rem(col, 2)


def device(z, x, y, core):
    return (z, (y * NX + x) * 2 + core)


def plane_peers(z, x, y, core):
    peers = [device(z, x, y, 1 - core)]
    for i in range(1, NX):
        for c in range(2):
            peers.append(device(z, lax.rem(x + i, NX), y, c))
            peers.append(device(z, x, lax.rem(y + i, NY), c))
    return peers


def remote(src, dst, send, recv, peer):
    return pltpu.make_async_remote_copy(
        src_ref=src, dst_ref=dst, send_sem=send, recv_sem=recv, device_id=peer, device_id_type=MESH
    )


def one_hot(index, height, live, target):
    rows = lax.broadcasted_iota(jnp.int32, (height, 256), 0)
    slots = lax.broadcasted_iota(jnp.int32, (height, 256), 1)
    hit = (target(rows) == index) & (slots < live)
    return jnp.where(hit, 1.0, 0.0).astype(BF16)


def slot_sums(hot, products, k):
    part = products[pl.ds(k, 256, stride=16), :]
    high = part.astype(BF16)
    low = (part - high.astype(F32)).astype(BF16)
    out = jnp.dot(hot, jnp.concatenate([high, low], axis=1), preferred_element_type=F32)
    return out[:, :128] + out[:, 128:]


def kernel(
    blocks, slot_rows, slot_cols, counts, table, reward_cols, cot, value_out, grad_out,
    stored, rows_s, cols_s, count_s, picks_s, rows_v, cols_v,
    tab, tabf, own_cot, full, sel, rew, w, wf, hot_rows, hot_cols,
    adjoint, forward, vsum, vtile, grads, gsum,
    abuf, bbuf, asum, bsum, fin, near, mid, far, relay,
    load_sem, block_sem, gsend, grecv, psend, precv, qsend, qrecv,
    zsend, zrecv, vsend, vrecv, fsend, frecv,
):
    z, x, y, core = position()
    partner = device(z, x, y, 1 - core)

    def along_z(step):
        return device(lax.rem(z + NZ + step, NZ), x, y, core)

    def at_z(step):
        return lax.rem(z + NZ + step, NZ)

    semaphore = pltpu.get_barrier_semaphore()
    peers = [along_z(2), along_z(-2), along_z(1), along_z(-1)] + plane_peers(z, x, y, core)
    for peer in peers:
        pl.semaphore_signal(semaphore, inc=1, device_id=peer, device_id_type=MESH)

    loads = [
        pltpu.make_async_copy(table, tab, load_sem.at[0]),
        pltpu.make_async_copy(reward_cols, picks_s, load_sem.at[1]),
        pltpu.make_async_copy(slot_rows, rows_s, load_sem.at[2]),
        pltpu.make_async_copy(slot_cols, cols_s, load_sem.at[3]),
        pltpu.make_async_copy(counts, count_s, load_sem.at[4]),
        pltpu.make_async_copy(slot_rows, rows_v, load_sem.at[5]),
        pltpu.make_async_copy(slot_cols, cols_v, load_sem.at[6]),
    ]
    cot_loads = [
        pltpu.make_async_copy(cot.at[:, pl.ds(t * 128, 128)], own_cot.at[t % 2, t // 2], load_sem.at[7 + t])
        for t in range(8)
    ]
    each = 256 // CHUNKS
    block_loads = [
        pltpu.make_async_copy(
            blocks.at[0, 0, pl.ds(i * each, each)], stored.at[pl.ds(i * each, each)], block_sem.at[i]
        )
        for i in range(CHUNKS)
    ]
    for load in loads[:1] + cot_loads + loads[1:] + block_loads:
        load.start()
    loads[0].wait()
    for j in range(64):
        tabf[pl.ds(j, 4, stride=64), :] = tab[:, j * 128 : (j + 1) * 128].astype(F32)
    for r in range(4):
        full[z * 4 + r] = tabf[r * 64 : (r + 1) * 64].astype(BF16)
    for load in cot_loads:
        load.wait()
    pl.semaphore_wait(semaphore, len(peers))

    def reward_copy(way, kind, half, receiving):
        sign = 1 if way == 0 else -1
        reach = (1, 2, 1, 2)[kind]
        origin = -sign * ((1, 2, 3, 4)[kind] if receiving else (0, 0, 2, 2)[kind])
        piece = full.at[pl.ds(at_z(origin) * 4 + half * 2, 2)]
        at = (way, kind, half)
        return remote(piece, piece, gsend.at[at], grecv.at[at], along_z(sign * reach))

    for kind in (1, 0):
        for half in (0, 1):
            for way in (0, 1):
                reward_copy(way, kind, half, False).start()

    first = [remote(own_cot.at[1 - core], w.at[y, x, core], psend.at[0, 0], precv.at[core, 0], partner)]
    for i in range(1, NX):
        tx = lax.rem(x + i * (1 - core), NX)
        ty = lax.rem(y + i * core, NY)
        for c in range(2):
            first.append(
                remote(own_cot.at[c], w.at[y, x, core], psend.at[i, c], precv.at[core, i], device(z, tx, ty, c))
            )
    for copy in first:
        copy.start()
    w[y, x, core] = own_cot[core]

    for load in loads[1:]:
        load.wait()
    live = count_s[0, 0]

    def block_row(at):
        half, a, b, t = at >> 6, (at >> 4) & 3, (at >> 2) & 3, at & 3
        tx, ty = jnp.where(half == 0, a, b), jnp.where(half == 0, b, a)
        return ((ty * NX + tx) * 2 + half) * 8 + t * 2 + core

    hot_rows[...] = one_hot(rows_v[0], 128, live, block_row)
    hot_cols[...] = one_hot(cols_v[0], 64, live, lambda at: at)

    remote(own_cot.at[0], w.at[y, x, 1 - core], psend.at[0, 0], precv.at[1 - core, 0], partner).wait_recv()
    for i in range(1, NX):
        for half in range(2):
            piece = w.at[lax.rem(y + NY - i * half, NY), lax.rem(x + NX - i * (1 - half), NX), half]
            remote(own_cot.at[0], piece, psend.at[0, 0], precv.at[half, i], partner).wait_recv()

    second = []
    for i in range(1, NX):
        row, column = w.at[y, :, 0], w.at[:, x, 1]
        second.append(
            remote(row, row, qsend.at[0, i], qrecv.at[0, i], device(z, x, lax.rem(y + i, NY), core))
        )
        second.append(
            remote(column, column, qsend.at[1, i], qrecv.at[1, i], device(z, lax.rem(x + i, NX), y, core))
        )
    for copy in second:
        copy.start()

    for half in (0, 1):
        for way in (0, 1):
            reward_copy(way, 1, half, True).wait_recv()
            reward_copy(way, 2, half, False).start()
            if half == way:
                reward_copy(way, 3, half, False).start()

    for load in block_loads:
        load.wait()

    for way in (0, 1):
        for half in (0, 1):
            reward_copy(way, 0, half, True).wait_recv()
            reward_copy(way, 2, half, True).wait_recv()
        reward_copy(way, 3, way, True).wait_recv()
    for k in range(16):
        sel[k * 64 : (k + 1) * 64] = full[picks_s[k]].astype(F32)
    for j in range(64):
        rew[j] = sel[pl.ds(j, 16, stride=64), :].astype(BF16)

    @pl.loop(0, 256, step=UNROLL)
    def _(start):
        for u in range(0, UNROLL, 2):
            s = start + u
            pair = stored[pl.ds(s, 2)].reshape(256, 128)
            left = jnp.concatenate([rew[cols_s[0, 0, s]], rew[cols_s[0, 0, s + 1]]], axis=0)
            out = lax.dot_general(left, pair, NT, preferred_element_type=F32)
            at = pl.multiple_of(s * 16, 32)
            forward[pl.ds(at, 16), :] = out[:16, :128]
            forward[pl.ds(at + 16, 16), :] = out[16:, 128:]

    for k in range(16):
        vsum[k * 128 : (k + 1) * 128] = slot_sums(hot_rows[...], forward, k)
    for i in range(128):
        vtile[i >> 6, (i >> 4) & 3, (i >> 2) & 3, i & 3] = vsum[pl.ds(i, 16, stride=128), :]

    value_first = []
    for i in range(1, NX):
        tx = lax.rem(x + i, NX)
        ty = lax.rem(y + i, NY)
        value_first.append(
            remote(vtile.at[0, tx], abuf.at[i - 1], vsend.at[0, i - 1], vrecv.at[0, i - 1], device(z, tx, y, core))
        )
        value_first.append(
            remote(vtile.at[1, ty], bbuf.at[i - 1], vsend.at[1, i - 1], vrecv.at[1, i - 1], device(z, x, ty, core))
        )
    for copy in value_first:
        copy.start()

    for i in range(1, NX):
        row, column = w.at[lax.rem(y + NY - i, NY), :, 0], w.at[:, lax.rem(x + NX - i, NX), 1]
        remote(row, row, qsend.at[0, i], qrecv.at[0, i], partner).wait_recv()
        remote(column, column, qsend.at[1, i], qrecv.at[1, i], partner).wait_recv()
    wf[...] = w[...].reshape(wf.shape)
    zero = jnp.zeros((16, 128), BF16)

    @pl.loop(0, 256, step=UNROLL)
    def _(start):
        for u in range(0, UNROLL, 2):
            s = start + u
            pair = stored[pl.ds(s, 2)].reshape(256, 128)
            w0 = wf[lax.div(rows_s[0, 0, s], 2)]
            w1 = wf[lax.div(rows_s[0, 0, s + 1], 2)]
            left = jnp.concatenate(
                [jnp.concatenate([w0, zero], axis=1), jnp.concatenate([zero, w1], axis=1)], axis=0
            )
            adjoint[pl.ds(pl.multiple_of(s * 16, 32), 32), :] = jnp.dot(left, pair, preferred_element_type=F32)

    for k in range(16):
        grads[k] = slot_sums(hot_cols[...], adjoint, k)

    def sign_of(way):
        return 1 if way == 0 else -1

    def far_copy(way):
        s = sign_of(way)
        return remote(
            grads.at[at_z(4) * 2 + way], far.at[way], zsend.at[way, 0], zrecv.at[way, 0], along_z(2 * s)
        )

    def mid_copy(way):
        s = sign_of(way)
        return remote(
            grads.at[pl.ds(at_z(3 * s) * 2, 2)], mid.at[way], zsend.at[way, 1], zrecv.at[way, 1], along_z(s)
        )

    def near_copy(way):
        s = sign_of(way)
        return remote(
            grads.at[pl.ds(at_z(s) * 2, 2)], near.at[0, way], zsend.at[way, 2], zrecv.at[way, 2], along_z(s)
        )

    def relay_copy(way):
        s = sign_of(way)
        return remote(relay.at[way], near.at[1, way], zsend.at[way, 3], zrecv.at[way, 3], along_z(2 * s))

    for copy in (far_copy, mid_copy, near_copy):
        for way in (0, 1):
            copy(way).start()

    for way in (0, 1):
        mid_copy(way).wait_recv()
        far_copy(way).wait_recv()
        s = sign_of(way)
        relay[way] = grads[pl.ds(at_z(2 * s) * 2, 2)] + mid[way]
        relay[way, way] = relay[way, way] + far[way]
        relay_copy(way).start()

    for copy in value_first:
        copy.wait_recv()
    asum[...] = vtile[0, x] + abuf[0] + abuf[1] + abuf[2]
    bsum[...] = vtile[1, y] + bbuf[0] + bbuf[1] + bbuf[2]

    value_second = []
    for i in range(1, NX):
        ty = lax.rem(y + i, NY)
        tx = lax.rem(x + i, NX)
        value_second.append(
            remote(asum.at[ty], fin.at[core, i], fsend.at[0, i], frecv.at[core, i], device(z, x, ty, 0))
        )
        value_second.append(
            remote(bsum.at[tx], fin.at[core, i], fsend.at[1, i], frecv.at[core, i], device(z, tx, y, 1))
        )
    for copy in value_second:
        copy.start()

    @pl.when(core == 0)
    def _():
        remote(bsum.at[x], fin.at[core, 0], fsend.at[0, 0], frecv.at[core, 0], partner).start()
        fin[core, 0] = asum[y]

    @pl.when(core == 1)
    def _():
        remote(asum.at[y], fin.at[core, 0], fsend.at[0, 0], frecv.at[core, 0], partner).start()
        fin[core, 0] = bsum[x]

    for way in (0, 1):
        near_copy(way).wait_recv()
        relay_copy(way).wait_recv()
    for r in (0, 1):
        gsum[r * 64 : (r + 1) * 64] = (
            grads[z * 2 + r] + near[0, 0, r] + near[0, 1, r] + near[1, 0, r] + near[1, 1, r]
        )
    for j in range(64):
        grad_out[:, j * 128 : (j + 1) * 128] = gsum[pl.ds(j, 2, stride=64), :]

    last = remote(asum.at[0], fin.at[1 - core, 0], fsend.at[0, 0], frecv.at[1 - core, 0], partner)
    last.wait_recv()
    for c in range(2):
        for i in range(1, NX):
            remote(asum.at[0], fin.at[c, i], fsend.at[0, i], frecv.at[c, i], partner).wait_recv()
    for t in range(8):
        p, h = t % 2, t // 2
        value_out[:, t * 128 : (t + 1) * 128] = fin[p, 0, h] + fin[p, 1, h] + fin[p, 2, h] + fin[p, 3, h]

    for way in (0, 1):
        for half in (0, 1):
            for kind in (0, 1, 2):
                reward_copy(way, kind, half, False).wait_send()
        reward_copy(way, 3, way, False).wait_send()
        for copy in (far_copy, mid_copy, near_copy, relay_copy):
            copy(way).wait_send()
    for copy in first + second + value_first + value_second + [last]:
        copy.wait_send()


def on_device(*operands):
    vmem = pl.BlockSpec(memory_space=pltpu.VMEM)
    dma = pltpu.SemaphoreType.DMA
    operands = [
        operand if operand.size == 1 else pltpu.with_memory_space_constraint(operand, pltpu.HBM)
        for operand in operands
    ]
    return pl.pallas_call(
        kernel,
        out_shape=(jax.ShapeDtypeStruct((16, 1024), F32), jax.ShapeDtypeStruct((2, 8192), F32)),
        in_specs=[pl.BlockSpec(memory_space=pltpu.HBM)] * 7,
        out_specs=(vmem, vmem),
        scratch_shapes=[
            pltpu.VMEM((256, 128, 128), BF16),
            pltpu.SMEM((1, 1, 256), jnp.int32),
            pltpu.SMEM((1, 1, 256), jnp.int32),
            pltpu.SMEM((1, 1), jnp.int32),
            pltpu.SMEM((16,), jnp.int32),
            pltpu.VMEM((1, 1, 256), jnp.int32),
            pltpu.VMEM((1, 1, 256), jnp.int32),
            pltpu.VMEM((4, 8192), BF16),
            pltpu.VMEM((256, 128), F32),
            pltpu.VMEM((2, 4, 16, 128), BF16),
            pltpu.VMEM((32, 64, 128), BF16),
            pltpu.VMEM((1024, 128), F32),
            pltpu.VMEM((64, 16, 128), BF16),
            pltpu.VMEM((NY, NX, 2, 4, 16, 128), BF16),
            pltpu.VMEM((128, 16, 128), BF16),
            pltpu.VMEM((128, 256), BF16),
            pltpu.VMEM((64, 256), BF16),
            pltpu.VMEM((4096, 128), F32),
            pltpu.VMEM((4096, 128), F32),
            pltpu.VMEM((2048, 128), F32),
            pltpu.VMEM((2, 4, 4, 4, 16, 128), F32),
            pltpu.VMEM((16, 64, 128), F32),
            pltpu.VMEM((128, 128), F32),
            pltpu.VMEM((3, 4, 4, 16, 128), F32),
            pltpu.VMEM((3, 4, 4, 16, 128), F32),
            pltpu.VMEM((4, 4, 16, 128), F32),
            pltpu.VMEM((4, 4, 16, 128), F32),
            pltpu.VMEM((2, 4, 4, 16, 128), F32),
            pltpu.VMEM((2, 2, 2, 64, 128), F32),
            pltpu.VMEM((2, 2, 64, 128), F32),
            pltpu.VMEM((2, 64, 128), F32),
            pltpu.VMEM((2, 2, 64, 128), F32),
            dma((15,)),
            dma((CHUNKS,)),
            dma((2, 4, 2)),
            dma((2, 4, 2)),
            dma((4, 2)),
            dma((2, 4)),
            dma((2, 4)),
            dma((2, 4)),
            dma((2, 4)),
            dma((2, 4)),
            dma((2, 3)),
            dma((2, 3)),
            dma((2, 4)),
            dma((2, 4)),
        ],
        compiler_params=pltpu.CompilerParams(
            collective_id=0, has_side_effects=True, vmem_limit_bytes=VMEM_BYTES
        ),
    )(*operands)


def solution(mesh):
    placed = (
        P("row", "col", None, None, None),
        P("row", "col", None),
        P("row", "col", None),
        P("row", "col"),
        P("row", "col"),
        P(),
        P(None, ("row", "col")),
    )
    return jax.shard_map(
        on_device,
        mesh=mesh,
        in_specs=placed,
        out_specs=(P(None, ("row", "col")), P("row", "col")),
        check_vma=False,
    )
```

```python
import functools

import jax
import jax.numpy as jnp
from jax import lax
from jax.experimental import pallas as pl
from jax.experimental.pallas import tpu as pltpu
from jax.sharding import PartitionSpec as P

F32 = jnp.float32
BF16 = jnp.bfloat16
MESH = pl.DeviceIdType.MESH
NT = (((1,), (1,)), ((), ()))
NZ = 8
NX = 4
NY = 4
VMEM_BYTES = 48 << 20
UNROLL = 128
TURN = 32
CHUNKS = 8


def position():
    z = lax.axis_index("row")
    col = lax.axis_index("col")
    return z, lax.rem(lax.div(col, 2), NX), lax.div(col, 2 * NX), lax.rem(col, 2)


def device(z, x, y, core):
    return (z, (y * NX + x) * 2 + core)


def plane_peers(z, x, y, core):
    peers = [device(z, x, y, 1 - core)]
    for i in range(1, NX):
        for c in range(2):
            peers.append(device(z, lax.rem(x + i, NX), y, c))
            peers.append(device(z, x, lax.rem(y + i, NY), c))
    return peers


def remote(src, dst, send, recv, peer):
    return pltpu.make_async_remote_copy(
        src_ref=src, dst_ref=dst, send_sem=send, recv_sem=recv, device_id=peer, device_id_type=MESH
    )


def one_hot(index, height, live, target):
    rows = lax.broadcasted_iota(jnp.int32, (height, 256), 0)
    slots = lax.broadcasted_iota(jnp.int32, (height, 256), 1)
    hit = (target(rows) == index) & (slots < live)
    return jnp.where(hit, 1.0, 0.0).astype(BF16)


def slot_sums(hot, products, k):
    part = products[pl.ds(k, 256, stride=16), :]
    high = part.astype(BF16)
    low = (part - high.astype(F32)).astype(BF16)
    out = jnp.dot(hot, jnp.concatenate([high, low], axis=1), preferred_element_type=F32)
    return out[:, :128] + out[:, 128:]


def kernel(
    blocks, slot_rows, slot_cols, counts, table, reward_cols, cot, value_out, grad_out,
    stored, turned, rows_s, cols_s, count_s, picks_s, rows_v, cols_v,
    tab, tabf, own_cot, full, sel, rew, w, wf, hot_rows, hot_cols,
    adjoint, forward, vsum, vtile, grads, gsum,
    abuf, bbuf, asum, bsum, fin, near, mid, far, relay,
    load_sem, block_sem, gsend, grecv, psend, precv, qsend, qrecv,
    zsend, zrecv, vsend, vrecv, fsend, frecv,
):
    z, x, y, core = position()
    partner = device(z, x, y, 1 - core)

    def along_z(step):
        return device(lax.rem(z + NZ + step, NZ), x, y, core)

    def at_z(step):
        return lax.rem(z + NZ + step, NZ)

    semaphore = pltpu.get_barrier_semaphore()
    peers = [along_z(2), along_z(-2), along_z(1), along_z(-1)] + plane_peers(z, x, y, core)
    for peer in peers:
        pl.semaphore_signal(semaphore, inc=1, device_id=peer, device_id_type=MESH)

    loads = [
        pltpu.make_async_copy(table, tab, load_sem.at[0]),
        pltpu.make_async_copy(reward_cols, picks_s, load_sem.at[1]),
        pltpu.make_async_copy(slot_rows, rows_s, load_sem.at[2]),
        pltpu.make_async_copy(slot_cols, cols_s, load_sem.at[3]),
        pltpu.make_async_copy(counts, count_s, load_sem.at[4]),
        pltpu.make_async_copy(slot_rows, rows_v, load_sem.at[5]),
        pltpu.make_async_copy(slot_cols, cols_v, load_sem.at[6]),
    ]
    cot_loads = [
        pltpu.make_async_copy(cot.at[:, pl.ds(t * 128, 128)], own_cot.at[t % 2, t // 2], load_sem.at[7 + t])
        for t in range(8)
    ]
    each = 256 // CHUNKS
    block_loads = [
        pltpu.make_async_copy(
            blocks.at[0, 0, pl.ds(i * each, each)], stored.at[pl.ds(i * each, each)], block_sem.at[i]
        )
        for i in range(CHUNKS)
    ]
    for load in loads[:1] + cot_loads + loads[1:] + block_loads:
        load.start()
    loads[0].wait()
    for j in range(64):
        tabf[pl.ds(j, 4, stride=64), :] = tab[:, j * 128 : (j + 1) * 128].astype(F32)
    for r in range(4):
        full[z * 4 + r] = tabf[r * 64 : (r + 1) * 64].astype(BF16)
    for load in cot_loads:
        load.wait()
    pl.semaphore_wait(semaphore, len(peers))

    def reward_copy(way, kind, half, receiving):
        sign = 1 if way == 0 else -1
        reach = (1, 2, 1, 2)[kind]
        origin = -sign * ((1, 2, 3, 4)[kind] if receiving else (0, 0, 2, 2)[kind])
        piece = full.at[pl.ds(at_z(origin) * 4 + half * 2, 2)]
        at = (way, kind, half)
        return remote(piece, piece, gsend.at[at], grecv.at[at], along_z(sign * reach))

    for kind in (1, 0):
        for half in (0, 1):
            for way in (0, 1):
                reward_copy(way, kind, half, False).start()

    first = [remote(own_cot.at[1 - core], w.at[y, x, core], psend.at[0, 0], precv.at[core, 0], partner)]
    for i in range(1, NX):
        tx = lax.rem(x + i * (1 - core), NX)
        ty = lax.rem(y + i * core, NY)
        for c in range(2):
            first.append(
                remote(own_cot.at[c], w.at[y, x, core], psend.at[i, c], precv.at[core, i], device(z, tx, ty, c))
            )
    for copy in first:
        copy.start()
    w[y, x, core] = own_cot[core]

    for load in loads[1:]:
        load.wait()
    live = count_s[0, 0]

    def block_row(at):
        half, a, b, t = at >> 6, (at >> 4) & 3, (at >> 2) & 3, at & 3
        tx, ty = jnp.where(half == 0, a, b), jnp.where(half == 0, b, a)
        return ((ty * NX + tx) * 2 + half) * 8 + t * 2 + core

    hot_rows[...] = one_hot(rows_v[0], 128, live, block_row)
    hot_cols[...] = one_hot(cols_v[0], 64, live, lambda at: at)

    def turn(start, stop):
        @pl.loop(start, stop, step=TURN)
        def _(at):
            for u in range(TURN):
                turned[at + u] = stored[at + u].T

    for load in block_loads[: CHUNKS // 2]:
        load.wait()
    turn(0, 128)
    remote(own_cot.at[0], w.at[y, x, 1 - core], psend.at[0, 0], precv.at[1 - core, 0], partner).wait_recv()
    for i in range(1, NX):
        for half in range(2):
            piece = w.at[lax.rem(y + NY - i * half, NY), lax.rem(x + NX - i * (1 - half), NX), half]
            remote(own_cot.at[0], piece, psend.at[0, 0], precv.at[half, i], partner).wait_recv()

    second = []
    for i in range(1, NX):
        row, column = w.at[y, :, 0], w.at[:, x, 1]
        second.append(
            remote(row, row, qsend.at[0, i], qrecv.at[0, i], device(z, x, lax.rem(y + i, NY), core))
        )
        second.append(
            remote(column, column, qsend.at[1, i], qrecv.at[1, i], device(z, lax.rem(x + i, NX), y, core))
        )
    for copy in second:
        copy.start()

    for load in block_loads[CHUNKS // 2 :]:
        load.wait()
    turn(128, 256)
    for half in (0, 1):
        for way in (0, 1):
            reward_copy(way, 1, half, True).wait_recv()
            reward_copy(way, 2, half, False).start()
            if half == way:
                reward_copy(way, 3, half, False).start()

    for way in (0, 1):
        for half in (0, 1):
            reward_copy(way, 0, half, True).wait_recv()
            reward_copy(way, 2, half, True).wait_recv()
        reward_copy(way, 3, way, True).wait_recv()
    for k in range(16):
        sel[k * 64 : (k + 1) * 64] = full[picks_s[k]].astype(F32)
    for j in range(64):
        rew[j] = sel[pl.ds(j, 16, stride=64), :].astype(BF16)

    zero = jnp.zeros((16, 128), BF16)

    def spread(a, b):
        return jnp.concatenate(
            [jnp.concatenate([a, zero], axis=1), jnp.concatenate([zero, b], axis=1)], axis=0
        )

    @pl.loop(0, 256, step=UNROLL)
    def _(start):
        for u in range(0, UNROLL, 2):
            s = start + u
            left = spread(rew[cols_s[0, 0, s]], rew[cols_s[0, 0, s + 1]])
            pair = turned[pl.ds(s, 2)].reshape(256, 128)
            forward[pl.ds(pl.multiple_of(s * 16, 32), 32), :] = jnp.dot(left, pair, preferred_element_type=F32)

    value_first = ([], [])
    for part in (0, 1):
        for k in range(part * 8, part * 8 + 8):
            vsum[k * 128 : (k + 1) * 128] = slot_sums(hot_rows[...], forward, k)
        for i in range(128):
            vtile[part, i >> 6, (i >> 4) & 3, (i >> 2) & 3, i & 3] = vsum[pl.ds(part * 1024 + i, 8, stride=128), :]
        for i in range(1, NX):
            tx = lax.rem(x + i, NX)
            ty = lax.rem(y + i, NY)
            for half, src, dst, peer in (
                (0, vtile.at[part, 0, tx], abuf, device(z, tx, y, core)),
                (1, vtile.at[part, 1, ty], bbuf, device(z, x, ty, core)),
            ):
                at = (part, half, i - 1)
                value_first[part].append(remote(src, dst.at[part, i - 1], vsend.at[at], vrecv.at[at], peer))
        for copy in value_first[part]:
            copy.start()

    for i in range(1, NX):
        row, column = w.at[lax.rem(y + NY - i, NY), :, 0], w.at[:, lax.rem(x + NX - i, NX), 1]
        remote(row, row, qsend.at[0, i], qrecv.at[0, i], partner).wait_recv()
        remote(column, column, qsend.at[1, i], qrecv.at[1, i], partner).wait_recv()
    wf[...] = w[...].reshape(wf.shape)
    @pl.loop(0, 256, step=UNROLL)
    def _(start):
        for u in range(0, UNROLL, 2):
            s = start + u
            left = spread(wf[lax.div(rows_s[0, 0, s], 2)], wf[lax.div(rows_s[0, 0, s + 1], 2)])
            pair = stored[pl.ds(s, 2)].reshape(256, 128)
            adjoint[pl.ds(pl.multiple_of(s * 16, 32), 32), :] = jnp.dot(left, pair, preferred_element_type=F32)

    def sign_of(way):
        return 1 if way == 0 else -1

    def far_copy(way):
        s = sign_of(way)
        return remote(
            grads.at[at_z(4) * 2 + way], far.at[way], zsend.at[way, 0], zrecv.at[way, 0], along_z(2 * s)
        )

    def mid_copy(way):
        s = sign_of(way)
        return remote(
            grads.at[pl.ds(at_z(3 * s) * 2, 2)], mid.at[way], zsend.at[way, 1], zrecv.at[way, 1], along_z(s)
        )

    def near_copy(way):
        s = sign_of(way)
        return remote(
            grads.at[pl.ds(at_z(s) * 2, 2)], near.at[0, way], zsend.at[way, 2], zrecv.at[way, 2], along_z(s)
        )

    def relay_copy(way):
        s = sign_of(way)
        return remote(relay.at[way], near.at[1, way], zsend.at[way, 3], zrecv.at[way, 3], along_z(2 * s))

    for step, ready in (
        (3, [(mid_copy, 0)]), (-3, [(mid_copy, 1)]), (4, [(far_copy, 0), (far_copy, 1)]),
        (1, [(near_copy, 0)]), (-1, [(near_copy, 1)]), (2, []), (-2, []), (0, []),
    ):
        for r in (0, 1):
            k = at_z(step) * 2 + r
            grads[k] = slot_sums(hot_cols[...], adjoint, k)
        for copy, way in ready:
            copy(way).start()

    value_second = []
    last = []
    for part in (0, 1):
        for copy in value_first[part]:
            copy.wait_recv()
        asum[part] = vtile[part, 0, x] + abuf[part, 0] + abuf[part, 1] + abuf[part, 2]
        bsum[part] = vtile[part, 1, y] + bbuf[part, 0] + bbuf[part, 1] + bbuf[part, 2]
        second_copies = []
        for i in range(1, NX):
            ty = lax.rem(y + i, NY)
            tx = lax.rem(x + i, NX)
            for half, src, peer in ((0, asum.at[part, ty], device(z, x, ty, 0)), (1, bsum.at[part, tx], device(z, tx, y, 1))):
                second_copies.append(
                    remote(src, fin.at[part, core, i], fsend.at[part, half, i], frecv.at[part, core, i], peer)
                )
        for copy in second_copies:
            copy.start()
        value_second += second_copies

        @pl.when(core == 0)
        def _():
            remote(
                bsum.at[part, x], fin.at[part, core, 0], fsend.at[part, 0, 0], frecv.at[part, core, 0], partner
            ).start()
            fin[part, core, 0] = asum[part, y]

        @pl.when(core == 1)
        def _():
            remote(
                asum.at[part, y], fin.at[part, core, 0], fsend.at[part, 0, 0], frecv.at[part, core, 0], partner
            ).start()
            fin[part, core, 0] = bsum[part, x]

        last.append(
            remote(
                asum.at[part, 0], fin.at[part, 1 - core, 0], fsend.at[part, 0, 0], frecv.at[part, 1 - core, 0], partner
            )
        )

    for way in (0, 1):
        mid_copy(way).wait_recv()
        far_copy(way).wait_recv()
        s = sign_of(way)
        relay[way] = grads[pl.ds(at_z(2 * s) * 2, 2)] + mid[way]
        relay[way, way] = relay[way, way] + far[way]
        relay_copy(way).start()

    for part in (0, 1):
        last[part].wait_recv()
        for c in range(2):
            for i in range(1, NX):
                remote(
                    asum.at[part, 0], fin.at[part, c, i], fsend.at[part, 0, i], frecv.at[part, c, i], partner
                ).wait_recv()
        for t in range(8):
            p, h = t % 2, t // 2
            value_out[part * 8 : part * 8 + 8, t * 128 : (t + 1) * 128] = (
                fin[part, p, 0, h] + fin[part, p, 1, h] + fin[part, p, 2, h] + fin[part, p, 3, h]
            )

    for way in (0, 1):
        near_copy(way).wait_recv()
        relay_copy(way).wait_recv()
    for r in (0, 1):
        gsum[r * 64 : (r + 1) * 64] = (
            grads[z * 2 + r] + near[0, 0, r] + near[0, 1, r] + near[1, 0, r] + near[1, 1, r]
        )
    for j in range(64):
        grad_out[:, j * 128 : (j + 1) * 128] = gsum[pl.ds(j, 2, stride=64), :]

    for way in (0, 1):
        for half in (0, 1):
            for kind in (0, 1, 2):
                reward_copy(way, kind, half, False).wait_send()
        reward_copy(way, 3, way, False).wait_send()
        for copy in (far_copy, mid_copy, near_copy, relay_copy):
            copy(way).wait_send()
    for copy in first + second + value_first[0] + value_first[1] + value_second + last:
        copy.wait_send()


def hand_on_kernel(value, grad, value_out, grad_out, sem):
    copies = [
        pltpu.make_async_copy(value, value_out, sem.at[0]),
        pltpu.make_async_copy(grad, grad_out, sem.at[1]),
    ]
    for copy in copies:
        copy.start()
    for copy in copies:
        copy.wait()


def hand_on(value, grad):
    vmem = pl.BlockSpec(memory_space=pltpu.VMEM)
    anywhere = pl.BlockSpec(memory_space=pl.ANY)
    return pl.pallas_call(
        hand_on_kernel,
        out_shape=(jax.ShapeDtypeStruct((16, 1024), F32), jax.ShapeDtypeStruct((2, 8192), F32)),
        in_specs=[vmem, vmem],
        out_specs=(anywhere, anywhere),
        scratch_shapes=[pltpu.SemaphoreType.DMA((2,))],
        compiler_params=pltpu.CompilerParams(vmem_limit_bytes=VMEM_BYTES),
    )(value, grad)


def on_device(*operands):
    vmem = pl.BlockSpec(memory_space=pltpu.VMEM)
    dma = pltpu.SemaphoreType.DMA
    operands = [
        operand if operand.size == 1 else pltpu.with_memory_space_constraint(operand, pltpu.HBM)
        for operand in operands
    ]
    value, grad = pl.pallas_call(
        kernel,
        out_shape=(jax.ShapeDtypeStruct((16, 1024), F32), jax.ShapeDtypeStruct((2, 8192), F32)),
        in_specs=[pl.BlockSpec(memory_space=pltpu.HBM)] * 7,
        out_specs=(vmem, vmem),
        scratch_shapes=[
            pltpu.VMEM((256, 128, 128), BF16),
            pltpu.VMEM((256, 128, 128), BF16),
            pltpu.SMEM((1, 1, 256), jnp.int32),
            pltpu.SMEM((1, 1, 256), jnp.int32),
            pltpu.SMEM((1, 1), jnp.int32),
            pltpu.SMEM((16,), jnp.int32),
            pltpu.VMEM((1, 1, 256), jnp.int32),
            pltpu.VMEM((1, 1, 256), jnp.int32),
            pltpu.VMEM((4, 8192), BF16),
            pltpu.VMEM((256, 128), F32),
            pltpu.VMEM((2, 4, 16, 128), BF16),
            pltpu.VMEM((32, 64, 128), BF16),
            pltpu.VMEM((1024, 128), F32),
            pltpu.VMEM((64, 16, 128), BF16),
            pltpu.VMEM((NY, NX, 2, 4, 16, 128), BF16),
            pltpu.VMEM((128, 16, 128), BF16),
            pltpu.VMEM((128, 256), BF16),
            pltpu.VMEM((64, 256), BF16),
            pltpu.VMEM((4096, 128), F32),
            pltpu.VMEM((4096, 128), F32),
            pltpu.VMEM((2048, 128), F32),
            pltpu.VMEM((2, 2, 4, 4, 4, 8, 128), F32),
            pltpu.VMEM((16, 64, 128), F32),
            pltpu.VMEM((128, 128), F32),
            pltpu.VMEM((2, 3, 4, 4, 8, 128), F32),
            pltpu.VMEM((2, 3, 4, 4, 8, 128), F32),
            pltpu.VMEM((2, 4, 4, 8, 128), F32),
            pltpu.VMEM((2, 4, 4, 8, 128), F32),
            pltpu.VMEM((2, 2, 4, 4, 8, 128), F32),
            pltpu.VMEM((2, 2, 2, 64, 128), F32),
            pltpu.VMEM((2, 2, 64, 128), F32),
            pltpu.VMEM((2, 64, 128), F32),
            pltpu.VMEM((2, 2, 64, 128), F32),
            dma((15,)),
            dma((CHUNKS,)),
            dma((2, 4, 2)),
            dma((2, 4, 2)),
            dma((4, 2)),
            dma((2, 4)),
            dma((2, 4)),
            dma((2, 4)),
            dma((2, 4)),
            dma((2, 4)),
            dma((2, 2, 3)),
            dma((2, 2, 3)),
            dma((2, 2, 4)),
            dma((2, 2, 4)),
        ],
        compiler_params=pltpu.CompilerParams(
            collective_id=0, has_side_effects=True, vmem_limit_bytes=VMEM_BYTES
        ),
    )(*operands)
    return hand_on(value, grad)


def solution(mesh):
    placed = (
        P("row", "col", None, None, None),
        P("row", "col", None),
        P("row", "col", None),
        P("row", "col"),
        P("row", "col"),
        P(),
        P(None, ("row", "col")),
    )
    return jax.shard_map(
        on_device,
        mesh=mesh,
        in_specs=placed,
        out_specs=(P(None, ("row", "col")), P("row", "col")),
        check_vma=False,
    )
```

```python
import functools

import jax
import jax.numpy as jnp
from jax import lax
from jax.experimental import pallas as pl
from jax.experimental.pallas import tpu as pltpu
from jax.sharding import PartitionSpec as P

F32 = jnp.float32
BF16 = jnp.bfloat16
MESH = pl.DeviceIdType.MESH
NT = (((1,), (1,)), ((), ()))
NZ = 8
NX = 4
NY = 4
VMEM_BYTES = 48 << 20
UNROLL = 128
TURN = 32
CHUNKS = 8


def position():
    z = lax.axis_index("row")
    col = lax.axis_index("col")
    return z, lax.rem(lax.div(col, 2), NX), lax.div(col, 2 * NX), lax.rem(col, 2)


def device(z, x, y, core):
    return (z, (y * NX + x) * 2 + core)


def plane_peers(z, x, y, core):
    peers = [device(z, x, y, 1 - core)]
    for i in range(1, NX):
        for c in range(2):
            peers.append(device(z, lax.rem(x + i, NX), y, c))
            peers.append(device(z, x, lax.rem(y + i, NY), c))
    return peers


def remote(src, dst, send, recv, peer):
    return pltpu.make_async_remote_copy(
        src_ref=src, dst_ref=dst, send_sem=send, recv_sem=recv, device_id=peer, device_id_type=MESH
    )


def one_hot(index, height, live, target):
    rows = lax.broadcasted_iota(jnp.int32, (height, 256), 0)
    slots = lax.broadcasted_iota(jnp.int32, (height, 256), 1)
    hit = (target(rows) == index) & (slots < live)
    return jnp.where(hit, 1.0, 0.0).astype(BF16)


def slot_sums(hot, products, k):
    part = products[pl.ds(k, 256, stride=16), :]
    high = part.astype(BF16)
    low = (part - high.astype(F32)).astype(BF16)
    out = jnp.dot(hot, jnp.concatenate([high, low], axis=1), preferred_element_type=F32)
    return out[:, :128] + out[:, 128:]


def kernel(
    blocks, slot_rows, slot_cols, counts, table, reward_cols, cot, value_out, grad_out,
    stored, turned, rows_s, cols_s, count_s, picks_s, rows_v, cols_v,
    tab, tabf, own_cot, full, sel, rew, w, wf, hot_rows, hot_cols,
    adjoint, forward, vsum, vtile, grads, gsum,
    abuf, bbuf, asum, bsum, fin, near, mid, far, relay,
    load_sem, block_sem, gsend, grecv, psend, precv, qsend, qrecv,
    zsend, zrecv, vsend, vrecv, fsend, frecv,
):
    z, x, y, core = position()
    partner = device(z, x, y, 1 - core)

    def along_z(step):
        return device(lax.rem(z + NZ + step, NZ), x, y, core)

    def at_z(step):
        return lax.rem(z + NZ + step, NZ)

    semaphore = pltpu.get_barrier_semaphore()
    peers = [along_z(2), along_z(-2), along_z(1), along_z(-1)] + plane_peers(z, x, y, core)
    for peer in peers:
        pl.semaphore_signal(semaphore, inc=1, device_id=peer, device_id_type=MESH)

    loads = [
        pltpu.make_async_copy(table, tab, load_sem.at[0]),
        pltpu.make_async_copy(reward_cols, picks_s, load_sem.at[1]),
        pltpu.make_async_copy(slot_rows, rows_s, load_sem.at[2]),
        pltpu.make_async_copy(slot_cols, cols_s, load_sem.at[3]),
        pltpu.make_async_copy(counts, count_s, load_sem.at[4]),
        pltpu.make_async_copy(slot_rows, rows_v, load_sem.at[5]),
        pltpu.make_async_copy(slot_cols, cols_v, load_sem.at[6]),
    ]
    cot_loads = [
        pltpu.make_async_copy(cot.at[:, pl.ds(t * 128, 128)], own_cot.at[t % 2, t // 2], load_sem.at[7 + t])
        for t in range(8)
    ]
    each = 256 // CHUNKS
    block_loads = [
        pltpu.make_async_copy(
            blocks.at[0, 0, pl.ds(i * each, each)], stored.at[pl.ds(i * each, each)], block_sem.at[i]
        )
        for i in range(CHUNKS)
    ]
    for load in loads[:1] + cot_loads + loads[1:] + block_loads:
        load.start()
    loads[0].wait()
    for j in range(64):
        tabf[pl.ds(j, 4, stride=64), :] = tab[:, j * 128 : (j + 1) * 128].astype(F32)
    for r in range(4):
        full[z * 4 + r] = tabf[r * 64 : (r + 1) * 64].astype(BF16)
    for load in cot_loads:
        load.wait()
    pl.semaphore_wait(semaphore, len(peers))

    def reward_copy(way, kind, half, receiving):
        sign = 1 if way == 0 else -1
        reach = (1, 2, 1, 2)[kind]
        origin = -sign * ((1, 2, 3, 4)[kind] if receiving else (0, 0, 2, 2)[kind])
        piece = full.at[pl.ds(at_z(origin) * 4 + half * 2, 2)]
        at = (way, kind, half)
        return remote(piece, piece, gsend.at[at], grecv.at[at], along_z(sign * reach))

    for kind in (1, 0):
        for half in (0, 1):
            for way in (0, 1):
                reward_copy(way, kind, half, False).start()

    first = [remote(own_cot.at[1 - core], w.at[y, x, core], psend.at[0, 0], precv.at[core, 0], partner)]
    for i in range(1, NX):
        tx = lax.rem(x + i * (1 - core), NX)
        ty = lax.rem(y + i * core, NY)
        for c in range(2):
            first.append(
                remote(own_cot.at[c], w.at[y, x, core], psend.at[i, c], precv.at[core, i], device(z, tx, ty, c))
            )
    for copy in first:
        copy.start()
    w[y, x, core] = own_cot[core]

    for load in loads[1:]:
        load.wait()
    live = count_s[0, 0]

    def block_row(at):
        half, a, b, t = at >> 6, (at >> 4) & 3, (at >> 2) & 3, at & 3
        tx, ty = jnp.where(half == 0, a, b), jnp.where(half == 0, b, a)
        return ((ty * NX + tx) * 2 + half) * 8 + t * 2 + core

    hot_rows[...] = one_hot(rows_v[0], 128, live, block_row)
    hot_cols[...] = one_hot(cols_v[0], 64, live, lambda at: at)

    def turn(start, stop):
        @pl.loop(start, stop, step=TURN)
        def _(at):
            for u in range(TURN):
                turned[at + u] = stored[at + u].T

    remote(own_cot.at[0], w.at[y, x, 1 - core], psend.at[0, 0], precv.at[1 - core, 0], partner).wait_recv()
    for i in range(1, NX):
        for half in range(2):
            piece = w.at[lax.rem(y + NY - i * half, NY), lax.rem(x + NX - i * (1 - half), NX), half]
            remote(own_cot.at[0], piece, psend.at[0, 0], precv.at[half, i], partner).wait_recv()

    second = []
    for i in range(1, NX):
        row, column = w.at[y, :, 0], w.at[:, x, 1]
        second.append(
            remote(row, row, qsend.at[0, i], qrecv.at[0, i], device(z, x, lax.rem(y + i, NY), core))
        )
        second.append(
            remote(column, column, qsend.at[1, i], qrecv.at[1, i], device(z, lax.rem(x + i, NX), y, core))
        )
    for copy in second:
        copy.start()

    for half in (0, 1):
        for way in (0, 1):
            reward_copy(way, 1, half, True).wait_recv()
            reward_copy(way, 2, half, False).start()
            if half == way:
                reward_copy(way, 3, half, False).start()

    for load in block_loads:
        load.wait()
    turn(0, 256)

    for way in (0, 1):
        for half in (0, 1):
            reward_copy(way, 0, half, True).wait_recv()
            reward_copy(way, 2, half, True).wait_recv()
        reward_copy(way, 3, way, True).wait_recv()
    for k in range(16):
        sel[k * 64 : (k + 1) * 64] = full[picks_s[k]].astype(F32)
    for j in range(64):
        rew[j] = sel[pl.ds(j, 16, stride=64), :].astype(BF16)

    zero = jnp.zeros((16, 128), BF16)

    def spread(a, b):
        return jnp.concatenate(
            [jnp.concatenate([a, zero], axis=1), jnp.concatenate([zero, b], axis=1)], axis=0
        )

    @pl.loop(0, 256, step=UNROLL)
    def _(start):
        for u in range(0, UNROLL, 2):
            s = start + u
            left = spread(rew[cols_s[0, 0, s]], rew[cols_s[0, 0, s + 1]])
            pair = turned[pl.ds(s, 2)].reshape(256, 128)
            forward[pl.ds(pl.multiple_of(s * 16, 32), 32), :] = jnp.dot(left, pair, preferred_element_type=F32)

    value_first = ([], [])
    for part in (0, 1):
        for k in range(part * 8, part * 8 + 8):
            vsum[k * 128 : (k + 1) * 128] = slot_sums(hot_rows[...], forward, k)
        for i in range(128):
            vtile[part, i >> 6, (i >> 4) & 3, (i >> 2) & 3, i & 3] = vsum[pl.ds(part * 1024 + i, 8, stride=128), :]
        for i in range(1, NX):
            tx = lax.rem(x + i, NX)
            ty = lax.rem(y + i, NY)
            for half, src, dst, peer in (
                (0, vtile.at[part, 0, tx], abuf, device(z, tx, y, core)),
                (1, vtile.at[part, 1, ty], bbuf, device(z, x, ty, core)),
            ):
                at = (part, half, i - 1)
                value_first[part].append(remote(src, dst.at[part, i - 1], vsend.at[at], vrecv.at[at], peer))
        for copy in value_first[part]:
            copy.start()

    for i in range(1, NX):
        row, column = w.at[lax.rem(y + NY - i, NY), :, 0], w.at[:, lax.rem(x + NX - i, NX), 1]
        remote(row, row, qsend.at[0, i], qrecv.at[0, i], partner).wait_recv()
        remote(column, column, qsend.at[1, i], qrecv.at[1, i], partner).wait_recv()
    wf[...] = w[...].reshape(wf.shape)
    @pl.loop(0, 256, step=UNROLL)
    def _(start):
        for u in range(0, UNROLL, 2):
            s = start + u
            left = spread(wf[lax.div(rows_s[0, 0, s], 2)], wf[lax.div(rows_s[0, 0, s + 1], 2)])
            pair = stored[pl.ds(s, 2)].reshape(256, 128)
            adjoint[pl.ds(pl.multiple_of(s * 16, 32), 32), :] = jnp.dot(left, pair, preferred_element_type=F32)

    def sign_of(way):
        return 1 if way == 0 else -1

    def far_copy(way):
        s = sign_of(way)
        return remote(
            grads.at[at_z(4) * 2 + way], far.at[way], zsend.at[way, 0], zrecv.at[way, 0], along_z(2 * s)
        )

    def mid_copy(way):
        s = sign_of(way)
        return remote(
            grads.at[pl.ds(at_z(3 * s) * 2, 2)], mid.at[way], zsend.at[way, 1], zrecv.at[way, 1], along_z(s)
        )

    def near_copy(way):
        s = sign_of(way)
        return remote(
            grads.at[pl.ds(at_z(s) * 2, 2)], near.at[0, way], zsend.at[way, 2], zrecv.at[way, 2], along_z(s)
        )

    def relay_copy(way):
        s = sign_of(way)
        return remote(relay.at[way], near.at[1, way], zsend.at[way, 3], zrecv.at[way, 3], along_z(2 * s))

    for step, ready in (
        (3, [(mid_copy, 0)]), (-3, [(mid_copy, 1)]), (4, [(far_copy, 0), (far_copy, 1)]),
        (1, [(near_copy, 0)]), (-1, [(near_copy, 1)]), (2, []), (-2, []), (0, []),
    ):
        for r in (0, 1):
            k = at_z(step) * 2 + r
            grads[k] = slot_sums(hot_cols[...], adjoint, k)
        for copy, way in ready:
            copy(way).start()

    value_second = []
    last = []
    for part in (0, 1):
        for copy in value_first[part]:
            copy.wait_recv()
        asum[part] = vtile[part, 0, x] + abuf[part, 0] + abuf[part, 1] + abuf[part, 2]
        bsum[part] = vtile[part, 1, y] + bbuf[part, 0] + bbuf[part, 1] + bbuf[part, 2]
        second_copies = []
        for i in range(1, NX):
            ty = lax.rem(y + i, NY)
            tx = lax.rem(x + i, NX)
            for half, src, peer in ((0, asum.at[part, ty], device(z, x, ty, 0)), (1, bsum.at[part, tx], device(z, tx, y, 1))):
                second_copies.append(
                    remote(src, fin.at[part, core, i], fsend.at[part, half, i], frecv.at[part, core, i], peer)
                )
        for copy in second_copies:
            copy.start()
        value_second += second_copies

        @pl.when(core == 0)
        def _():
            remote(
                bsum.at[part, x], fin.at[part, core, 0], fsend.at[part, 0, 0], frecv.at[part, core, 0], partner
            ).start()
            fin[part, core, 0] = asum[part, y]

        @pl.when(core == 1)
        def _():
            remote(
                asum.at[part, y], fin.at[part, core, 0], fsend.at[part, 0, 0], frecv.at[part, core, 0], partner
            ).start()
            fin[part, core, 0] = bsum[part, x]

        last.append(
            remote(
                asum.at[part, 0], fin.at[part, 1 - core, 0], fsend.at[part, 0, 0], frecv.at[part, 1 - core, 0], partner
            )
        )

    for way in (0, 1):
        mid_copy(way).wait_recv()
        far_copy(way).wait_recv()
        s = sign_of(way)
        relay[way] = grads[pl.ds(at_z(2 * s) * 2, 2)] + mid[way]
        relay[way, way] = relay[way, way] + far[way]
        relay_copy(way).start()

    for part in (0, 1):
        last[part].wait_recv()
        for c in range(2):
            for i in range(1, NX):
                remote(
                    asum.at[part, 0], fin.at[part, c, i], fsend.at[part, 0, i], frecv.at[part, c, i], partner
                ).wait_recv()
        for t in range(8):
            p, h = t % 2, t // 2
            value_out[part * 8 : part * 8 + 8, t * 128 : (t + 1) * 128] = (
                fin[part, p, 0, h] + fin[part, p, 1, h] + fin[part, p, 2, h] + fin[part, p, 3, h]
            )

    for way in (0, 1):
        near_copy(way).wait_recv()
        relay_copy(way).wait_recv()
    for r in (0, 1):
        gsum[r * 64 : (r + 1) * 64] = (
            grads[z * 2 + r] + near[0, 0, r] + near[0, 1, r] + near[1, 0, r] + near[1, 1, r]
        )
    for j in range(64):
        grad_out[:, j * 128 : (j + 1) * 128] = gsum[pl.ds(j, 2, stride=64), :]

    for way in (0, 1):
        for half in (0, 1):
            for kind in (0, 1, 2):
                reward_copy(way, kind, half, False).wait_send()
        reward_copy(way, 3, way, False).wait_send()
        for copy in (far_copy, mid_copy, near_copy, relay_copy):
            copy(way).wait_send()
    for copy in first + second + value_first[0] + value_first[1] + value_second + last:
        copy.wait_send()


def hand_on_kernel(value, grad, value_out, grad_out, sem):
    copies = [
        pltpu.make_async_copy(value, value_out, sem.at[0]),
        pltpu.make_async_copy(grad, grad_out, sem.at[1]),
    ]
    for copy in copies:
        copy.start()
    for copy in copies:
        copy.wait()


def hand_on(value, grad):
    vmem = pl.BlockSpec(memory_space=pltpu.VMEM)
    anywhere = pl.BlockSpec(memory_space=pl.ANY)
    return pl.pallas_call(
        hand_on_kernel,
        out_shape=(jax.ShapeDtypeStruct((16, 1024), F32), jax.ShapeDtypeStruct((2, 8192), F32)),
        in_specs=[vmem, vmem],
        out_specs=(anywhere, anywhere),
        scratch_shapes=[pltpu.SemaphoreType.DMA((2,))],
        compiler_params=pltpu.CompilerParams(vmem_limit_bytes=VMEM_BYTES),
    )(value, grad)


def on_device(*operands):
    vmem = pl.BlockSpec(memory_space=pltpu.VMEM)
    dma = pltpu.SemaphoreType.DMA
    operands = [
        operand if operand.size == 1 else pltpu.with_memory_space_constraint(operand, pltpu.HBM)
        for operand in operands
    ]
    value, grad = pl.pallas_call(
        kernel,
        out_shape=(jax.ShapeDtypeStruct((16, 1024), F32), jax.ShapeDtypeStruct((2, 8192), F32)),
        in_specs=[pl.BlockSpec(memory_space=pltpu.HBM)] * 7,
        out_specs=(vmem, vmem),
        scratch_shapes=[
            pltpu.VMEM((256, 128, 128), BF16),
            pltpu.VMEM((256, 128, 128), BF16),
            pltpu.SMEM((1, 1, 256), jnp.int32),
            pltpu.SMEM((1, 1, 256), jnp.int32),
            pltpu.SMEM((1, 1), jnp.int32),
            pltpu.SMEM((16,), jnp.int32),
            pltpu.VMEM((1, 1, 256), jnp.int32),
            pltpu.VMEM((1, 1, 256), jnp.int32),
            pltpu.VMEM((4, 8192), BF16),
            pltpu.VMEM((256, 128), F32),
            pltpu.VMEM((2, 4, 16, 128), BF16),
            pltpu.VMEM((32, 64, 128), BF16),
            pltpu.VMEM((1024, 128), F32),
            pltpu.VMEM((64, 16, 128), BF16),
            pltpu.VMEM((NY, NX, 2, 4, 16, 128), BF16),
            pltpu.VMEM((128, 16, 128), BF16),
            pltpu.VMEM((128, 256), BF16),
            pltpu.VMEM((64, 256), BF16),
            pltpu.VMEM((4096, 128), F32),
            pltpu.VMEM((4096, 128), F32),
            pltpu.VMEM((2048, 128), F32),
            pltpu.VMEM((2, 2, 4, 4, 4, 8, 128), F32),
            pltpu.VMEM((16, 64, 128), F32),
            pltpu.VMEM((128, 128), F32),
            pltpu.VMEM((2, 3, 4, 4, 8, 128), F32),
            pltpu.VMEM((2, 3, 4, 4, 8, 128), F32),
            pltpu.VMEM((2, 4, 4, 8, 128), F32),
            pltpu.VMEM((2, 4, 4, 8, 128), F32),
            pltpu.VMEM((2, 2, 4, 4, 8, 128), F32),
            pltpu.VMEM((2, 2, 2, 64, 128), F32),
            pltpu.VMEM((2, 2, 64, 128), F32),
            pltpu.VMEM((2, 64, 128), F32),
            pltpu.VMEM((2, 2, 64, 128), F32),
            dma((15,)),
            dma((CHUNKS,)),
            dma((2, 4, 2)),
            dma((2, 4, 2)),
            dma((4, 2)),
            dma((2, 4)),
            dma((2, 4)),
            dma((2, 4)),
            dma((2, 4)),
            dma((2, 4)),
            dma((2, 2, 3)),
            dma((2, 2, 3)),
            dma((2, 2, 4)),
            dma((2, 2, 4)),
        ],
        compiler_params=pltpu.CompilerParams(
            collective_id=0, has_side_effects=True, vmem_limit_bytes=VMEM_BYTES
        ),
    )(*operands)
    return hand_on(value, grad)


def solution(mesh):
    placed = (
        P("row", "col", None, None, None),
        P("row", "col", None),
        P("row", "col", None),
        P("row", "col"),
        P("row", "col"),
        P(),
        P(None, ("row", "col")),
    )
    return jax.shard_map(
        on_device,
        mesh=mesh,
        in_specs=placed,
        out_specs=(P(None, ("row", "col")), P("row", "col")),
        check_vma=False,
    )
```

```python
import functools

import jax
import jax.numpy as jnp
from jax import lax
from jax.experimental import pallas as pl
from jax.experimental.pallas import tpu as pltpu
from jax.sharding import PartitionSpec as P

F32 = jnp.float32
BF16 = jnp.bfloat16
MESH = pl.DeviceIdType.MESH
NT = (((1,), (1,)), ((), ()))
NZ = 8
NX = 4
NY = 4
VMEM_BYTES = 48 << 20
UNROLL = 128
TURN = 32
CHUNKS = 8


def position():
    z = lax.axis_index("row")
    col = lax.axis_index("col")
    return z, lax.rem(lax.div(col, 2), NX), lax.div(col, 2 * NX), lax.rem(col, 2)


def device(z, x, y, core):
    return (z, (y * NX + x) * 2 + core)


def plane_peers(z, x, y, core):
    peers = [device(z, x, y, 1 - core)]
    for i in range(1, NX):
        for c in range(2):
            peers.append(device(z, lax.rem(x + i, NX), y, c))
            peers.append(device(z, x, lax.rem(y + i, NY), c))
    return peers


def remote(src, dst, send, recv, peer):
    return pltpu.make_async_remote_copy(
        src_ref=src, dst_ref=dst, send_sem=send, recv_sem=recv, device_id=peer, device_id_type=MESH
    )


def one_hot(index, height, live, target):
    rows = lax.broadcasted_iota(jnp.int32, (height, 256), 0)
    slots = lax.broadcasted_iota(jnp.int32, (height, 256), 1)
    hit = (target(rows) == index) & (slots < live)
    return jnp.where(hit, 1.0, 0.0).astype(BF16)


def slot_sums(hot, products, k):
    part = products[pl.ds(k, 256, stride=16), :]
    high = part.astype(BF16)
    low = (part - high.astype(F32)).astype(BF16)
    out = jnp.dot(hot, jnp.concatenate([high, low], axis=1), preferred_element_type=F32)
    return out[:, :128] + out[:, 128:]


def kernel(
    blocks, slot_rows, slot_cols, counts, table, reward_cols, cot, value_out, grad_out,
    stored, turned, rows_s, cols_s, count_s, picks_s, rows_v, cols_v,
    tab, tabf, own_cot, full, sel, rew, w, wf, hot_rows, hot_cols,
    adjoint, forward, vsum, vtile, grads, gsum,
    abuf, bbuf, asum, bsum, fin, near, mid, far, relay,
    load_sem, block_sem, gsend, grecv, psend, precv, qsend, qrecv,
    zsend, zrecv, vsend, vrecv, fsend, frecv,
):
    z, x, y, core = position()
    partner = device(z, x, y, 1 - core)

    def along_z(step):
        return device(lax.rem(z + NZ + step, NZ), x, y, core)

    def at_z(step):
        return lax.rem(z + NZ + step, NZ)

    semaphore = pltpu.get_barrier_semaphore()
    peers = [along_z(2), along_z(-2), along_z(1), along_z(-1)] + plane_peers(z, x, y, core)
    for peer in peers:
        pl.semaphore_signal(semaphore, inc=1, device_id=peer, device_id_type=MESH)

    loads = [
        pltpu.make_async_copy(table, tab, load_sem.at[0]),
        pltpu.make_async_copy(reward_cols, picks_s, load_sem.at[1]),
        pltpu.make_async_copy(slot_rows, rows_s, load_sem.at[2]),
        pltpu.make_async_copy(slot_cols, cols_s, load_sem.at[3]),
        pltpu.make_async_copy(counts, count_s, load_sem.at[4]),
        pltpu.make_async_copy(slot_rows, rows_v, load_sem.at[5]),
        pltpu.make_async_copy(slot_cols, cols_v, load_sem.at[6]),
    ]
    cot_loads = [
        pltpu.make_async_copy(cot.at[:, pl.ds(t * 128, 128)], own_cot.at[t % 2, t // 2], load_sem.at[7 + t])
        for t in range(8)
    ]
    each = 256 // CHUNKS
    block_loads = [
        pltpu.make_async_copy(
            blocks.at[0, 0, pl.ds(i * each, each)], stored.at[pl.ds(i * each, each)], block_sem.at[i]
        )
        for i in range(CHUNKS)
    ]
    for load in loads[:1] + cot_loads + loads[1:] + block_loads:
        load.start()
    loads[0].wait()
    for j in range(64):
        tabf[pl.ds(j, 4, stride=64), :] = tab[:, j * 128 : (j + 1) * 128].astype(F32)
    for r in range(4):
        full[z * 4 + r] = tabf[r * 64 : (r + 1) * 64].astype(BF16)
    for load in cot_loads:
        load.wait()
    pl.semaphore_wait(semaphore, len(peers))

    def reward_copy(way, kind, half, receiving):
        sign = 1 if way == 0 else -1
        reach = (1, 2, 1, 2)[kind]
        origin = -sign * ((1, 2, 3, 4)[kind] if receiving else (0, 0, 2, 2)[kind])
        piece = full.at[pl.ds(at_z(origin) * 4 + half * 2, 2)]
        at = (way, kind, half)
        return remote(piece, piece, gsend.at[at], grecv.at[at], along_z(sign * reach))

    for kind in (1, 0):
        for half in (0, 1):
            for way in (0, 1):
                reward_copy(way, kind, half, False).start()

    first = [remote(own_cot.at[1 - core], w.at[y, x, core], psend.at[0, 0], precv.at[core, 0], partner)]
    for i in range(1, NX):
        tx = lax.rem(x + i * (1 - core), NX)
        ty = lax.rem(y + i * core, NY)
        for c in range(2):
            first.append(
                remote(own_cot.at[c], w.at[y, x, core], psend.at[i, c], precv.at[core, i], device(z, tx, ty, c))
            )
    for copy in first:
        copy.start()
    w[y, x, core] = own_cot[core]

    def turn(start, stop):
        @pl.loop(start, stop, step=TURN)
        def _(at):
            for u in range(TURN):
                turned[at + u] = stored[at + u].T

    for half in (0, 1):
        for way in (0, 1):
            reward_copy(way, 1, half, True).wait_recv()
            reward_copy(way, 2, half, False).start()
            if half == way:
                reward_copy(way, 3, half, False).start()

    remote(own_cot.at[0], w.at[y, x, 1 - core], psend.at[0, 0], precv.at[1 - core, 0], partner).wait_recv()
    for i in range(1, NX):
        for half in range(2):
            piece = w.at[lax.rem(y + NY - i * half, NY), lax.rem(x + NX - i * (1 - half), NX), half]
            remote(own_cot.at[0], piece, psend.at[0, 0], precv.at[half, i], partner).wait_recv()

    second = []
    for i in range(1, NX):
        row, column = w.at[y, :, 0], w.at[:, x, 1]
        second.append(
            remote(row, row, qsend.at[0, i], qrecv.at[0, i], device(z, x, lax.rem(y + i, NY), core))
        )
        second.append(
            remote(column, column, qsend.at[1, i], qrecv.at[1, i], device(z, lax.rem(x + i, NX), y, core))
        )
    for copy in second:
        copy.start()

    for load in block_loads:
        load.wait()
    turn(0, 256)

    for load in loads[1:]:
        load.wait()
    live = count_s[0, 0]

    def block_row(at):
        half, a, b, t = at >> 6, (at >> 4) & 3, (at >> 2) & 3, at & 3
        tx, ty = jnp.where(half == 0, a, b), jnp.where(half == 0, b, a)
        return ((ty * NX + tx) * 2 + half) * 8 + t * 2 + core

    hot_rows[...] = one_hot(rows_v[0], 128, live, block_row)
    hot_cols[...] = one_hot(cols_v[0], 64, live, lambda at: at)

    for way in (0, 1):
        for half in (0, 1):
            reward_copy(way, 0, half, True).wait_recv()
            reward_copy(way, 2, half, True).wait_recv()
        reward_copy(way, 3, way, True).wait_recv()
    for k in range(16):
        sel[k * 64 : (k + 1) * 64] = full[picks_s[k]].astype(F32)
    for j in range(64):
        rew[j] = sel[pl.ds(j, 16, stride=64), :].astype(BF16)

    zero = jnp.zeros((16, 128), BF16)

    def spread(a, b):
        return jnp.concatenate(
            [jnp.concatenate([a, zero], axis=1), jnp.concatenate([zero, b], axis=1)], axis=0
        )

    @pl.loop(0, 256, step=UNROLL)
    def _(start):
        for u in range(0, UNROLL, 2):
            s = start + u
            left = spread(rew[cols_s[0, 0, s]], rew[cols_s[0, 0, s + 1]])
            pair = turned[pl.ds(s, 2)].reshape(256, 128)
            forward[pl.ds(pl.multiple_of(s * 16, 32), 32), :] = jnp.dot(left, pair, preferred_element_type=F32)

    value_first = ([], [])
    for part in (0, 1):
        for k in range(part * 8, part * 8 + 8):
            vsum[k * 128 : (k + 1) * 128] = slot_sums(hot_rows[...], forward, k)
        for i in range(128):
            vtile[part, i >> 6, (i >> 4) & 3, (i >> 2) & 3, i & 3] = vsum[pl.ds(part * 1024 + i, 8, stride=128), :]
        for i in (2, 1, 3):
            tx = lax.rem(x + i, NX)
            ty = lax.rem(y + i, NY)
            for half, src, dst, peer in (
                (0, vtile.at[part, 0, tx], abuf, device(z, tx, y, core)),
                (1, vtile.at[part, 1, ty], bbuf, device(z, x, ty, core)),
            ):
                at = (part, half, i - 1)
                value_first[part].append(remote(src, dst.at[part, i - 1], vsend.at[at], vrecv.at[at], peer))
        for copy in value_first[part]:
            copy.start()

    for i in range(1, NX):
        row, column = w.at[lax.rem(y + NY - i, NY), :, 0], w.at[:, lax.rem(x + NX - i, NX), 1]
        remote(row, row, qsend.at[0, i], qrecv.at[0, i], partner).wait_recv()
        remote(column, column, qsend.at[1, i], qrecv.at[1, i], partner).wait_recv()
    wf[...] = w[...].reshape(wf.shape)
    @pl.loop(0, 256, step=UNROLL)
    def _(start):
        for u in range(0, UNROLL, 2):
            s = start + u
            left = spread(wf[lax.div(rows_s[0, 0, s], 2)], wf[lax.div(rows_s[0, 0, s + 1], 2)])
            pair = stored[pl.ds(s, 2)].reshape(256, 128)
            adjoint[pl.ds(pl.multiple_of(s * 16, 32), 32), :] = jnp.dot(left, pair, preferred_element_type=F32)

    def sign_of(way):
        return 1 if way == 0 else -1

    def far_copy(way):
        s = sign_of(way)
        return remote(
            grads.at[at_z(4) * 2 + way], far.at[way], zsend.at[way, 0], zrecv.at[way, 0], along_z(2 * s)
        )

    def mid_copy(way):
        s = sign_of(way)
        return remote(
            grads.at[pl.ds(at_z(3 * s) * 2, 2)], mid.at[way], zsend.at[way, 1], zrecv.at[way, 1], along_z(s)
        )

    def near_copy(way):
        s = sign_of(way)
        return remote(
            grads.at[pl.ds(at_z(s) * 2, 2)], near.at[0, way], zsend.at[way, 2], zrecv.at[way, 2], along_z(s)
        )

    def relay_copy(way):
        s = sign_of(way)
        return remote(relay.at[way], near.at[1, way], zsend.at[way, 3], zrecv.at[way, 3], along_z(2 * s))

    for step, ready in (
        (3, [(mid_copy, 0)]), (-3, [(mid_copy, 1)]), (4, [(far_copy, 0), (far_copy, 1)]),
        (1, [(near_copy, 0)]), (-1, [(near_copy, 1)]), (2, []), (-2, []), (0, []),
    ):
        for r in (0, 1):
            k = at_z(step) * 2 + r
            grads[k] = slot_sums(hot_cols[...], adjoint, k)
        for copy, way in ready:
            copy(way).start()

    value_second = []
    last = []
    for part in (0, 1):
        for copy in value_first[part]:
            copy.wait_recv()
        asum[part] = vtile[part, 0, x] + abuf[part, 0] + abuf[part, 1] + abuf[part, 2]
        bsum[part] = vtile[part, 1, y] + bbuf[part, 0] + bbuf[part, 1] + bbuf[part, 2]
        second_copies = []
        for i in range(1, NX):
            ty = lax.rem(y + i, NY)
            tx = lax.rem(x + i, NX)
            for half, src, peer in ((0, asum.at[part, ty], device(z, x, ty, 0)), (1, bsum.at[part, tx], device(z, tx, y, 1))):
                second_copies.append(
                    remote(src, fin.at[part, core, i], fsend.at[part, half, i], frecv.at[part, core, i], peer)
                )
        for copy in second_copies:
            copy.start()
        value_second += second_copies

        @pl.when(core == 0)
        def _():
            remote(
                bsum.at[part, x], fin.at[part, core, 0], fsend.at[part, 0, 0], frecv.at[part, core, 0], partner
            ).start()
            fin[part, core, 0] = asum[part, y]

        @pl.when(core == 1)
        def _():
            remote(
                asum.at[part, y], fin.at[part, core, 0], fsend.at[part, 0, 0], frecv.at[part, core, 0], partner
            ).start()
            fin[part, core, 0] = bsum[part, x]

        last.append(
            remote(
                asum.at[part, 0], fin.at[part, 1 - core, 0], fsend.at[part, 0, 0], frecv.at[part, 1 - core, 0], partner
            )
        )

    for way in (0, 1):
        mid_copy(way).wait_recv()
        far_copy(way).wait_recv()
        s = sign_of(way)
        relay[way] = grads[pl.ds(at_z(2 * s) * 2, 2)] + mid[way]
        relay[way, way] = relay[way, way] + far[way]
        relay_copy(way).start()

    for part in (0, 1):
        last[part].wait_recv()
        for c in range(2):
            for i in range(1, NX):
                remote(
                    asum.at[part, 0], fin.at[part, c, i], fsend.at[part, 0, i], frecv.at[part, c, i], partner
                ).wait_recv()
        for t in range(8):
            p, h = t % 2, t // 2
            value_out[part * 8 : part * 8 + 8, t * 128 : (t + 1) * 128] = (
                fin[part, p, 0, h] + fin[part, p, 1, h] + fin[part, p, 2, h] + fin[part, p, 3, h]
            )

    for way in (0, 1):
        near_copy(way).wait_recv()
        relay_copy(way).wait_recv()
    for r in (0, 1):
        gsum[r * 64 : (r + 1) * 64] = (
            grads[z * 2 + r] + near[0, 0, r] + near[0, 1, r] + near[1, 0, r] + near[1, 1, r]
        )
    for j in range(64):
        grad_out[:, j * 128 : (j + 1) * 128] = gsum[pl.ds(j, 2, stride=64), :]

    for way in (0, 1):
        for half in (0, 1):
            for kind in (0, 1, 2):
                reward_copy(way, kind, half, False).wait_send()
        reward_copy(way, 3, way, False).wait_send()
        for copy in (far_copy, mid_copy, near_copy, relay_copy):
            copy(way).wait_send()
    for copy in first + second + value_first[0] + value_first[1] + value_second + last:
        copy.wait_send()


def hand_on_kernel(value, grad, value_out, grad_out, sem):
    copies = [
        pltpu.make_async_copy(value, value_out, sem.at[0]),
        pltpu.make_async_copy(grad, grad_out, sem.at[1]),
    ]
    for copy in copies:
        copy.start()
    for copy in copies:
        copy.wait()


def hand_on(value, grad):
    vmem = pl.BlockSpec(memory_space=pltpu.VMEM)
    anywhere = pl.BlockSpec(memory_space=pl.ANY)
    return pl.pallas_call(
        hand_on_kernel,
        out_shape=(jax.ShapeDtypeStruct((16, 1024), F32), jax.ShapeDtypeStruct((2, 8192), F32)),
        in_specs=[vmem, vmem],
        out_specs=(anywhere, anywhere),
        scratch_shapes=[pltpu.SemaphoreType.DMA((2,))],
        compiler_params=pltpu.CompilerParams(vmem_limit_bytes=VMEM_BYTES),
    )(value, grad)


def on_device(*operands):
    vmem = pl.BlockSpec(memory_space=pltpu.VMEM)
    dma = pltpu.SemaphoreType.DMA
    operands = [
        operand if operand.size == 1 else pltpu.with_memory_space_constraint(operand, pltpu.HBM)
        for operand in operands
    ]
    value, grad = pl.pallas_call(
        kernel,
        out_shape=(jax.ShapeDtypeStruct((16, 1024), F32), jax.ShapeDtypeStruct((2, 8192), F32)),
        in_specs=[pl.BlockSpec(memory_space=pltpu.HBM)] * 7,
        out_specs=(vmem, vmem),
        scratch_shapes=[
            pltpu.VMEM((256, 128, 128), BF16),
            pltpu.VMEM((256, 128, 128), BF16),
            pltpu.SMEM((1, 1, 256), jnp.int32),
            pltpu.SMEM((1, 1, 256), jnp.int32),
            pltpu.SMEM((1, 1), jnp.int32),
            pltpu.SMEM((16,), jnp.int32),
            pltpu.VMEM((1, 1, 256), jnp.int32),
            pltpu.VMEM((1, 1, 256), jnp.int32),
            pltpu.VMEM((4, 8192), BF16),
            pltpu.VMEM((256, 128), F32),
            pltpu.VMEM((2, 4, 16, 128), BF16),
            pltpu.VMEM((32, 64, 128), BF16),
            pltpu.VMEM((1024, 128), F32),
            pltpu.VMEM((64, 16, 128), BF16),
            pltpu.VMEM((NY, NX, 2, 4, 16, 128), BF16),
            pltpu.VMEM((128, 16, 128), BF16),
            pltpu.VMEM((128, 256), BF16),
            pltpu.VMEM((64, 256), BF16),
            pltpu.VMEM((4096, 128), F32),
            pltpu.VMEM((4096, 128), F32),
            pltpu.VMEM((2048, 128), F32),
            pltpu.VMEM((2, 2, 4, 4, 4, 8, 128), F32),
            pltpu.VMEM((16, 64, 128), F32),
            pltpu.VMEM((128, 128), F32),
            pltpu.VMEM((2, 3, 4, 4, 8, 128), F32),
            pltpu.VMEM((2, 3, 4, 4, 8, 128), F32),
            pltpu.VMEM((2, 4, 4, 8, 128), F32),
            pltpu.VMEM((2, 4, 4, 8, 128), F32),
            pltpu.VMEM((2, 2, 4, 4, 8, 128), F32),
            pltpu.VMEM((2, 2, 2, 64, 128), F32),
            pltpu.VMEM((2, 2, 64, 128), F32),
            pltpu.VMEM((2, 64, 128), F32),
            pltpu.VMEM((2, 2, 64, 128), F32),
            dma((15,)),
            dma((CHUNKS,)),
            dma((2, 4, 2)),
            dma((2, 4, 2)),
            dma((4, 2)),
            dma((2, 4)),
            dma((2, 4)),
            dma((2, 4)),
            dma((2, 4)),
            dma((2, 4)),
            dma((2, 2, 3)),
            dma((2, 2, 3)),
            dma((2, 2, 4)),
            dma((2, 2, 4)),
        ],
        compiler_params=pltpu.CompilerParams(
            collective_id=0, has_side_effects=True, vmem_limit_bytes=VMEM_BYTES
        ),
    )(*operands)
    return hand_on(value, grad)


def solution(mesh):
    placed = (
        P("row", "col", None, None, None),
        P("row", "col", None),
        P("row", "col", None),
        P("row", "col"),
        P("row", "col"),
        P(),
        P(None, ("row", "col")),
    )
    return jax.shard_map(
        on_device,
        mesh=mesh,
        in_specs=placed,
        out_specs=(P(None, ("row", "col")), P("row", "col")),
        check_vma=False,
    )
```
